512 devices in a mesh: expert: 64 (over x, y_hi, z), tensor: 8 (over y_lo, core).
Axes of the slice: x: 4, y: 8 (y_hi: 2, y_lo: 4; y = y_hi * 4 + y_lo), z: 8, core: 2. Of those that a mesh axis runs over, the one named last changes fastest.
Arguments:
- tokens: bfloat16 [1024, 3584], P('expert', 'tensor'), may hold values from -6 to 6
- grad_out: bfloat16 [1024, 3584], P('expert', 'tensor'), may hold values from -6 to 6
- gate_weights: bfloat16 [1024, 8], P('expert'), may hold values from 0.099609375 to 1
- routing: int32 [1024, 8], P('expert'), may hold values from 0 to 63, all different within a row; in each aligned block of 16 rows (0 to 15, 16 to 31, ...) at most 3 rows name the same one
- w_gate: bfloat16 [64, 3584, 1024], P('expert', None, 'tensor'), may hold values from -0.09375 to 0.09375
- w_up: bfloat16 [64, 3584, 1024], P('expert', None, 'tensor'), may hold values from -0.09375 to 0.09375
- w_down: bfloat16 [64, 1024, 3584], P('expert', 'tensor'), may hold values from -0.1875 to 0.1875
Outputs:
- grad_tokens: bfloat16 [1024, 3584], P('expert', 'tensor')
- grad_gate: bfloat16 [64, 3584, 1024], P('expert', None, 'tensor')
- grad_up: bfloat16 [64, 3584, 1024], P('expert', None, 'tensor')
The draws below stay inside these ranges and needn't reach their ends.
Inputs may be any that keep to these rules, and one draw needn't show every extreme that they name: `routing`: each row names 8 different experts; within the rows of one device (aligned blocks of 16 rows) no expert is named by more than 3 rows.
All inputs are finite; a program needn't handle non-finite values.
Results may differ from the reference program's by a relative error of at most 0.014.
Values may be sent and summed in bfloat16 or wider, within the bound.
No kernel may reach another device: no remote copies, remote signals or barrier semaphores. Data moves between devices by JAX's collectives and lax.ppermute only.
A program may use at most 64 MiB of HBM per device.

```python
import math
import jax
import jax.numpy as jnp
import numpy as np
from jax import lax

D = 3584
FF = 1024
TOP = 8
TOK_DEV = 16
EXPERTS = 64
CAP = 3
SLOTS = 192
TOKENS = 1024
N_TENSOR = 8


def block_levels(stream_key, shape, pieces, least, high):
    def one(dim, shards_of):
        steps = jax.random.uniform(jax.random.fold_in(jax.random.fold_in(stream_key, 6), dim), (shards_of,), jnp.float32, least / len(pieces), high / len(pieces))
        return jnp.repeat(jnp.exp(steps), shape[dim] // shards_of).reshape((-1,) + (1,) * (len(shape) - dim - 1))

    factor_of = one(*pieces[0])
    for cut in pieces[1:]:
        factor_of = factor_of * one(*cut)
    return factor_of


def assign_block(rng, own, number, rows, amount, top, limit, slope):
    ranking = jax.random.permutation(rng, amount)
    heavy_load, ordinary = portions_of(amount, rows * top, limit, slope, True), portions_of(amount, rows * top, limit, slope, False)
    places = jnp.arange(amount)

    def named(sizes, turn):
        used = int((sizes > 0).sum())
        fixed = max(1, used // 4)
        shifted = fixed + (places - fixed + turn * (used - fixed)) % max(1, amount - fixed)
        return jnp.zeros((amount,), jnp.int32).at[ranking[jnp.where(places < fixed, places, shifted)]].set(jnp.asarray(sizes, jnp.int32))

    sizes = jnp.where(number % 4 == 0, named(heavy_load, number // 4), named(ordinary, number - number // 4 - 1))
    mixed = jax.random.permutation(jax.random.fold_in(own, 3), amount)
    donor, receiver = mixed[0:amount // 2 * 2:2], mixed[1:amount // 2 * 2:2]
    slack = jnp.minimum(sizes[donor] - 1, limit - sizes[receiver]) // 2
    slack = jnp.where((donor == ranking[0]) | (receiver == ranking[0]) | (sizes[receiver] == 0), 0, jnp.maximum(slack, 0))
    shifted = jax.random.randint(jax.random.fold_in(own, 4), (amount // 2,), 0, 1 << 20) % (slack + 1)
    sizes = sizes.at[donor].add(-shifted).at[receiver].add(shifted)
    members = jnp.searchsorted(jnp.cumsum(sizes), jnp.arange(rows * top), side="right").astype(jnp.int32)
    grid = members.reshape(top, rows).T
    grid = grid[jax.random.permutation(jax.random.fold_in(own, 1), rows)]
    turn = jax.random.randint(jax.random.fold_in(own, 2), (rows, 1), 0, top)
    return jnp.take_along_axis(grid, (jnp.arange(top)[None, :] + turn) % top, axis=1)


def portions_of(amount, total, reach, lean, full):
    weights = [(1 << 20) // math.isqrt(standing ** lean) + 1 for standing in range(1, amount + 1)]
    largest = reach if full else min(reach, max(-(-total // amount), total * weights[0] // sum(weights)))
    least = 1 if total - largest >= amount - 1 else 0
    given, surplus = [largest] + [least] * (amount - 1), total - largest - least * (amount - 1)
    while surplus > 0:
        free = [i for i in range(1, amount) if given[i] < largest] or [i for i in range(1, amount) if given[i] < reach]
        pool, budget = sum([weights[i] for i in free]), surplus
        for i in free:
            extra = min(reach - given[i], max(1, budget * weights[i] // pool), surplus)
            given[i] = given[i] + extra
            surplus = surplus - extra
    return np.array(given)


def bell_draw(own_key, dims, width, most, split=(), kind=jnp.bfloat16):
    drawn = jax.random.normal(own_key, dims, jnp.float32) * width
    if len(split) > 0:
        drawn = block_levels(own_key, dims, split, -0.22, 0.18) * drawn
    return jnp.clip(drawn, min=-most, max=most).astype(kind)


def setup_inputs(seed: int = 0) -> dict:
    seeds = jax.random.split(jax.random.key(seed), 8)
    tokens = bell_draw(seeds[0], (TOKENS, D), 1.0, 6.0, ((0, 64), (1, 8)))
    grad_out = bell_draw(seeds[1], (TOKENS, D), 1.0, 6.0, ((0, 64), (1, 8)))
    gate_weights = jnp.clip(0.099609375 + 0.9003906 * jax.random.uniform(seeds[2], (TOKENS, TOP), jnp.float32) ** block_levels(seeds[2], (TOKENS, TOP), ((0, 64),), -0.2, 0.2), 0.099609375, 1.0).astype(jnp.bfloat16)
    routing_keys = jax.random.split(jax.random.fold_in(seeds[3], 1), TOKENS // TOK_DEV)
    routing_turns = jax.random.permutation(jax.random.fold_in(seeds[3], 3), TOKENS // TOK_DEV)
    routing = jax.vmap(lambda own, number: assign_block(jax.random.fold_in(seeds[3], 2), own, number, TOK_DEV, EXPERTS, TOP, CAP, 2))(routing_keys, routing_turns).reshape((TOKENS, TOP))
    w_gate = bell_draw(seeds[4], (EXPERTS, D, FF), D ** -0.5, 0.09375, ((0, 64), (2, 8)))
    w_up = bell_draw(seeds[5], (EXPERTS, D, FF), D ** -0.5, 0.09375, ((0, 64), (2, 8)))
    w_down = bell_draw(seeds[6], (EXPERTS, FF, D), FF ** -0.5, 0.1875, ((0, 64), (1, 8)))
    return {"tokens": tokens, "grad_out": grad_out, "gate_weights": gate_weights, "routing": routing, "w_gate": w_gate, "w_up": w_up, "w_down": w_down}


def expert_step(carry, expert_id, tokens, grad_out, gate_weights, routing, w_gate, w_up, w_down):
    hit = routing == expert_id
    picked = jnp.any(hit, axis=1)
    weight = jnp.sum(jnp.where(hit, gate_weights.astype(jnp.float32), jnp.float32(0.0)), axis=1)
    sort_keys = jnp.where(picked, 0, 1).astype(jnp.int32)
    order = jnp.argsort(sort_keys, stable=True)[:SLOTS].astype(jnp.int32)
    valid = picked[order]
    rows_x = tokens[order]
    rows_dy = grad_out[order]
    scale = jnp.where(valid, weight[order], jnp.float32(0.0))
    wg = w_gate[expert_id]
    wu = w_up[expert_id]
    wd = w_down[expert_id]
    pre_gate = jnp.dot(rows_x, wg, preferred_element_type=jnp.float32)
    pre_up = jnp.dot(rows_x, wu, preferred_element_type=jnp.float32)
    back_act = jnp.dot(rows_dy, wd.T, preferred_element_type=jnp.float32)
    sig = jax.nn.sigmoid(pre_gate)
    d_gate = (scale[:, None] * back_act * pre_up * sig * (1.0 + pre_gate * (1.0 - sig))).astype(jnp.bfloat16)
    d_up = (scale[:, None] * back_act * pre_gate * sig).astype(jnp.bfloat16)
    grad_g = jnp.dot(rows_x.T, d_gate, preferred_element_type=jnp.float32).astype(jnp.bfloat16)
    grad_u = jnp.dot(rows_x.T, d_up, preferred_element_type=jnp.float32).astype(jnp.bfloat16)
    hidden = FF // N_TENSOR
    dg32 = d_gate.astype(jnp.float32).reshape(SLOTS, N_TENSOR, hidden)
    du32 = d_up.astype(jnp.float32).reshape(SLOTS, N_TENSOR, hidden)
    wg32 = wg.astype(jnp.float32).reshape(D, N_TENSOR, hidden)
    wu32 = wu.astype(jnp.float32).reshape(D, N_TENSOR, hidden)
    parts = jnp.einsum('rnh,dnh->nrd', dg32, wg32) + jnp.einsum('rnh,dnh->nrd', du32, wu32)
    rounded = lax.optimization_barrier(parts.astype(jnp.bfloat16)).astype(jnp.float32)
    contrib = jnp.sum(rounded, axis=0) * valid[:, None].astype(jnp.float32)
    carry = carry.at[order].add(contrib)
    return carry, (grad_g, grad_u)


def reference(tokens, grad_out, gate_weights, routing, w_gate, w_up, w_down):
    def step(carry, expert_id):
        return expert_step(carry, expert_id, tokens, grad_out, gate_weights, routing, w_gate, w_up, w_down)

    start = jnp.zeros((TOKENS, D), jnp.float32)
    total, grads = lax.scan(step, start, jnp.arange(EXPERTS, dtype=jnp.int32))
    return total.astype(jnp.bfloat16), grads[0], grads[1]
```

```python
import functools

import jax
import jax.numpy as jnp
from jax import lax
from jax.experimental import pallas as pl
from jax.experimental.pallas import tpu as pltpu
from jax.sharding import Mesh, PartitionSpec as P

BF = jnp.bfloat16
F32 = jnp.float32
AXES = ("x", "yh", "z", "yl", "core")
XZ = ("x", "z")
COL = ("yh", "yl")
LANES = 128
HALF = 64
VMEM_LIMIT = 40 * 1024 * 1024


def axis_sizes(experts, tensor):
    if (experts, tensor) == (64, 8):
        return (4, 2, 8, 4, 2)
    assert experts % 4 == 0 and tensor % 4 == 0
    return (experts // 4, 2, 2, tensor // 2, 2)


class Plan:
    def __init__(self, sizes, tok_rows, picks, part_w):
        self.nx, self.nyh, self.nz, self.nyl, self.nc = sizes
        self.tok, self.picks, self.part_w = tok_rows, picks, part_w
        experts = self.nx * self.nyh * self.nz
        self.cap = 3 * tok_rows * picks // (2 * experts)
        self.nq = self.nx * self.nz
        self.nb = self.nyh * self.nyl
        self.full = part_w // LANES
        assert part_w == self.full * LANES + HALF
        self.groups = 2 * self.full + 1
        self.lanes = self.nb * tok_rows
        self.c = self.nyh * self.cap
        self.cp = -(-self.c // 8) * 8
        self.grp = self.nyl * self.c
        self.rows = self.nq * self.c
        self.msg = self.groups * self.grp + self.cp
        self.ntail = self.nyl // 2
        self.ret = self.full * self.grp + self.ntail * self.cp
        self.half_d = self.nyl * part_w
        self.pre = self.groups * tok_rows + 2 * picks
        self.fin = (self.full + 1) * tok_rows


def iota(shape, dim):
    return lax.broadcasted_iota(jnp.int32, shape, dim)


def call(kernel, outs, args, name, scratch=(), flops=0):
    vm = pl.BlockSpec(memory_space=pltpu.VMEM)
    size = sum(a.size * a.dtype.itemsize for a in args) + sum(
        jnp.dtype(o[1]).itemsize * functools.reduce(lambda a, b: a * b, o[0]) for o in outs
    )
    shapes = [jax.ShapeDtypeStruct(s, d) for s, d in outs]
    return pl.pallas_call(
        kernel,
        out_shape=shapes,
        in_specs=[vm] * len(args),
        out_specs=[vm] * len(outs),
        scratch_shapes=list(scratch),
        compiler_params=pltpu.CompilerParams(vmem_limit_bytes=VMEM_LIMIT),
        cost_estimate=pl.CostEstimate(flops=flops, bytes_accessed=size, transcendentals=0),
        name=name,
    )(*args)


def pack_kernel(p, x_ref, dy_ref, route_ref, gate_ref, out_ref):
    block = lax.axis_index("yh") * p.nyl + lax.axis_index("yl")
    top = p.full * LANES
    low = (iota((HALF, LANES), 1) == iota((HALF, LANES), 0)).astype(BF)
    high = (iota((HALF, LANES), 1) == iota((HALF, LANES), 0) + HALF).astype(BF)
    mixed = jnp.dot(x_ref[:, top:], low, preferred_element_type=F32) + jnp.dot(
        dy_ref[:, top:], high, preferred_element_type=F32
    )
    lanes = (iota((p.tok, LANES), 1) == iota((p.tok, LANES), 0) + block * p.tok).astype(BF)
    meta = jnp.concatenate(
        [route_ref[...].astype(F32), gate_ref[...].astype(F32)], axis=0
    ).astype(BF)
    placed = jnp.dot(meta, lanes, preferred_element_type=F32).astype(BF)
    t = p.tok
    for b in range(p.nb):
        for j in range(p.full):
            out_ref[b, j * t : (j + 1) * t, :] = x_ref[:, j * LANES : (j + 1) * LANES]
            k = p.full + 1 + j
            out_ref[b, k * t : (k + 1) * t, :] = dy_ref[:, j * LANES : (j + 1) * LANES]
        out_ref[b, p.full * t : (p.full + 1) * t, :] = mixed.astype(BF)
        out_ref[b, p.groups * t :, :] = placed


def slot_target(p, rows_per, count):
    r = iota((rows_per * count, p.lanes), 0)
    l = iota((rows_per * count, p.lanes), 1)
    c, piece = r % rows_per, r // rows_per
    b = l // p.tok
    fits = (piece == b % p.nyl) & (c // p.cap == b // p.nyl) & (c < p.c)
    return jnp.where(fits, c % p.cap, -2).astype(F32)


def one_hot(p, ranks, target):
    rows = target.shape[0]
    eq = ranks[:, None, :] == target[None, :, :]
    return jnp.where(eq, 1.0, 0.0).astype(F32).reshape(p.nq * rows, p.lanes).astype(BF)


def dispatch_kernel(p, in_ref, out_ref, rank_ref):
    yh = lax.axis_index("yh")
    t = p.tok
    meta = in_ref[0, p.groups * t :, :].astype(F32)
    for b in range(1, p.nb):
        meta = meta + in_ref[b, p.groups * t :, :].astype(F32)
    q = iota((p.nq, p.lanes), 0)
    expert = (((q // p.nz) * p.nyh + yh) * p.nz + q % p.nz).astype(F32)
    hit = jnp.zeros((p.nq, p.lanes), F32)
    gate = jnp.zeros((p.nq, p.lanes), F32)
    for k in range(p.picks):
        same = meta[k : k + 1, : p.lanes] == expert
        hit = hit + jnp.where(same, 1.0, 0.0)
        gate = gate + jnp.where(same, meta[p.picks + k : p.picks + k + 1, : p.lanes], 0.0)
    a, b = iota((p.lanes, p.lanes), 0), iota((p.lanes, p.lanes), 1)
    before = jnp.where((a < b) & (a // t == b // t), 1.0, 0.0).astype(BF)
    rank = jnp.dot(hit.astype(BF), before, preferred_element_type=F32)
    ranks = jnp.where(hit > 0.5, rank, -1.0)
    rank_ref[...] = ranks
    pick = one_hot(p, ranks, slot_target(p, p.c, p.nyl))
    for g in range(p.groups):
        feats = in_ref[:, g * t : (g + 1) * t, :].reshape(p.lanes, LANES)
        rows = jnp.dot(pick, feats, preferred_element_type=F32)
        out_ref[:, g * p.grp : (g + 1) * p.grp, :] = rows.astype(BF).reshape(p.nq, p.grp, LANES)
    target = slot_target(p, p.cp, 1)
    eq = ranks[:, None, :] == target[None, :, :]
    gates = jnp.where(eq, jnp.broadcast_to(gate[:, None, :], eq.shape), 0.0)
    gates = gates.reshape(p.nq * p.cp, p.lanes).astype(BF)
    spread = jnp.dot(gates, jnp.ones((p.lanes, LANES), BF), preferred_element_type=F32)
    out_ref[:, p.groups * p.grp :, :] = spread.astype(BF).reshape(p.nq, p.cp, LANES)


def project_kernel(p, in_ref, wgu_ref, wd_ref, x_ref, own_ref, sib_ref, gate_ref, flat, dy):
    for s in range(p.nq):
        flat[s * p.msg : (s + 1) * p.msg, :] = in_ref[s].astype(F32)

    def piece(row):
        return jnp.concatenate(
            [flat[pl.ds(row + c, p.nq, stride=p.msg), :] for c in range(p.c)], axis=0
        )

    for j in range(p.full):
        for yl in range(p.nyl):
            at = (j * p.nyl + yl) * LANES
            x_ref[:, at : at + LANES] = piece(j * p.grp + yl * p.c).astype(BF)
            dy[:, at : at + LANES] = piece((p.full + 1 + j) * p.grp + yl * p.c).astype(BF)
    left = iota((p.rows, LANES), 1) < HALF
    for u in range(p.ntail):
        at = (p.full * p.nyl + u) * LANES
        a = piece(p.full * p.grp + 2 * u * p.c)
        b = piece(p.full * p.grp + (2 * u + 1) * p.c)
        x_ref[:, at : at + LANES] = jnp.where(left, a, pltpu.roll(b, HALF, 1)).astype(BF)
        dy[:, at : at + LANES] = jnp.where(left, pltpu.roll(a, HALF, 1), b).astype(BF)
    gate_ref[...] = piece(p.groups * p.grp)
    pre = jnp.dot(x_ref[...], wgu_ref[...], preferred_element_type=F32)
    back = jnp.dot(dy[...], wd_ref[...], preferred_element_type=F32)
    two = 2 * LANES
    own_ref[:, :two] = pre[:, :two]
    sib_ref[:, :two] = pre[:, two:]
    own_ref[:, two:] = back[:, :LANES]
    sib_ref[:, two:] = back[:, LANES:]


def act_kernel(own_ref, got_ref, gate_ref, d_ref):
    pre_gate = own_ref[:, :LANES] + got_ref[:, :LANES]
    pre_up = own_ref[:, LANES : 2 * LANES] + got_ref[:, LANES : 2 * LANES]
    back = own_ref[:, 2 * LANES :] + got_ref[:, 2 * LANES :]
    sig = 1.0 / (1.0 + jnp.exp(-pre_gate))
    scaled = gate_ref[...] * back
    d_ref[:, :LANES] = (scaled * pre_up * sig * (1.0 + pre_gate * (1.0 - sig))).astype(BF)
    d_ref[:, LANES:] = (scaled * pre_gate * sig).astype(BF)


def back_kernel(p, own_ref, sib_ref, wgu_ref, out_ref, flat):
    two = 2 * LANES
    nt = (((1,), (1,)), ((), ()))
    tail = p.full * p.grp
    for u in range(p.ntail):
        for c in range(p.c, p.cp):
            flat[pl.ds(tail + u * p.cp + c, p.nq, stride=p.ret), :] = jnp.zeros((p.nq, LANES), F32)
    chunks = p.full * p.nyl + p.ntail
    for k in range(chunks):
        at = k * LANES
        part = lax.dot_general(
            own_ref[...], wgu_ref[at : at + LANES, :two], nt, preferred_element_type=F32
        ) + lax.dot_general(
            sib_ref[...], wgu_ref[at : at + LANES, two:], nt, preferred_element_type=F32
        )
        base = k * p.c if k < p.full * p.nyl else tail + (k - p.full * p.nyl) * p.cp
        for c in range(p.c):
            flat[pl.ds(base + c, p.nq, stride=p.ret), :] = part[c * p.nq : (c + 1) * p.nq, :]
    for s in range(p.nq):
        out_ref[s] = flat[s * p.ret : (s + 1) * p.ret, :].astype(BF)


def combine_kernel(p, in_ref, rank_ref, out_ref):
    ranks = rank_ref[...]
    t = p.tok
    tn = (((0,), (0,)), ((), ()))
    pick = one_hot(p, ranks, slot_target(p, p.c, p.nyl))
    for g in range(p.full):
        rows = in_ref[:, g * p.grp : (g + 1) * p.grp, :].reshape(p.nq * p.grp, LANES)
        total = lax.dot_general(pick, rows, tn, preferred_element_type=F32)
        out_ref[:, g * t : (g + 1) * t, :] = total.astype(BF).reshape(p.nb, t, LANES)
    pick = one_hot(p, ranks, slot_target(p, p.cp, p.ntail))
    rows = in_ref[:, p.full * p.grp :, :].reshape(p.nq * p.ntail * p.cp, LANES)
    total = lax.dot_general(pick, rows, tn, preferred_element_type=F32).astype(BF)
    for b in range(p.nb):
        src = (b // p.nyl) * p.nyl + (b % p.nyl) // 2
        out_ref[b, p.full * t :, :] = total[src * t : (src + 1) * t, :]


def finish_kernel(p, in_ref, out_ref):
    odd = lax.axis_index("yl") % 2
    total = in_ref[0].astype(F32)
    for b in range(1, p.nb):
        total = total + in_ref[b].astype(F32)
    t = p.tok
    for j in range(p.full):
        out_ref[:, j * LANES : (j + 1) * LANES] = total[j * t : (j + 1) * t, :].astype(BF)
    tail = total[p.full * t :, :]
    tail = jnp.where(odd == 1, pltpu.roll(tail, HALF, 1), tail)
    out_ref[:, p.full * LANES :] = tail[:, :HALF].astype(BF)


def grads_kernel(p, x_ref, own_ref, sib_ref, mine_ref, other_ref):
    tn = (((0,), (0,)), ((), ()))

    def put(yl, at, size, src, got, k):
        mine_ref[k, yl, at : at + size, :] = got[src : src + size, k * LANES : (k + 1) * LANES]

    def put_other(yl, at, size, src, got):
        other_ref[yl, at : at + size, :] = got[src : src + size, :]

    for k in range(p.full * p.nyl + p.ntail):
        x = x_ref[:, k * LANES : (k + 1) * LANES]
        mine = lax.dot_general(x, own_ref[...], tn, preferred_element_type=F32).astype(BF)
        other = lax.dot_general(x, sib_ref[...], tn, preferred_element_type=F32).astype(BF)
        if k < p.full * p.nyl:
            spots = [(k % p.nyl, (k // p.nyl) * LANES, LANES, 0)]
        else:
            u = k - p.full * p.nyl
            spots = [(2 * u + h, p.full * LANES, HALF, h * HALF) for h in range(2)]
        for spot in spots:
            put(*spot, mine, 0)
            put(*spot, mine, 1)
            put_other(*spot, other)


def assemble_kernel(p, mine_ref, got_ref, gate_ref, up_ref):
    core = lax.axis_index("core")
    for yl in range(p.nyl):
        gate_ref[yl, core] = mine_ref[0, yl]
        up_ref[yl, core] = mine_ref[1, yl]
        gate_ref[yl, 1 - core] = got_ref[yl, :, :LANES]
        up_ref[yl, 1 - core] = got_ref[yl, :, LANES:]


def lane_tiles(p, w):
    top = p.full * LANES
    n = w.shape[-1]
    tiles = w[:, :top].reshape(p.nyl, p.full, LANES, n).transpose(1, 0, 2, 3).reshape(-1, n)
    return jnp.concatenate([tiles, w[:, top:].reshape(-1, n)], axis=0)


def body(sizes, tokens, grad_out, gate_weights, routing, w_gate, w_up, w_down):
    p = Plan(sizes, *routing.shape, tokens.shape[1])
    swap = [(0, 1), (1, 0)]
    core = lax.axis_index("core")
    bind = functools.partial

    def exchange(v):
        return lax.ppermute(v, "core", swap)

    def all_to_all(v, axes):
        return lax.all_to_all(v, axes, split_axis=0, concat_axis=0, tiled=True)

    (pre,) = call(
        bind(pack_kernel, p),
        [((p.nb, p.pre, LANES), BF)],
        (tokens, grad_out, routing.T, gate_weights.T),
        "pack",
    )
    column = all_to_all(pre, COL)

    w_gate, w_up, w_down = lax.optimization_barrier((w_gate, w_up, w_down, pre))[:3]
    shape = (p.nyl, p.nc, p.part_w, LANES)
    weights = jnp.stack(
        [w_gate[0].reshape(shape), w_up[0].reshape(shape), w_down[0].T.reshape(shape)]
    )
    mine = lax.dynamic_index_in_dim(weights, core, axis=2, keepdims=False)
    theirs = exchange(lax.dynamic_index_in_dim(weights, 1 - core, axis=2, keepdims=False))
    wgu = lane_tiles(p, jnp.concatenate([mine[0], mine[1], theirs[0], theirs[1]], axis=-1))
    wd = lane_tiles(p, jnp.concatenate([mine[2], theirs[2]], axis=-1))

    sent, ranks = call(
        bind(dispatch_kernel, p),
        [((p.nq, p.msg, LANES), BF), ((p.nq, p.lanes), F32)],
        (column,),
        "dispatch",
    )
    received = all_to_all(sent, XZ)
    rows_x, own, sib, gates = call(
        bind(project_kernel, p),
        [
            ((p.rows, p.half_d), BF),
            ((p.rows, 3 * LANES), F32),
            ((p.rows, 3 * LANES), F32),
            ((p.rows, LANES), F32),
        ],
        (received, wgu, wd),
        "project",
        scratch=[pltpu.VMEM((p.nq * p.msg, LANES), F32), pltpu.VMEM((p.rows, p.half_d), BF)],
    )
    (d_own,) = call(
        act_kernel, [((p.rows, 2 * LANES), BF)], (own, exchange(sib), gates), "act"
    )
    d_sib = exchange(d_own)
    (back,) = call(
        bind(back_kernel, p),
        [((p.nq, p.ret, LANES), BF)],
        (d_own, d_sib, wgu),
        "back",
        scratch=[pltpu.VMEM((p.nq * p.ret, LANES), F32)],
    )
    returned = all_to_all(back, XZ)
    rows_x, d_own, d_sib = lax.optimization_barrier((rows_x, d_own, d_sib, back))[:3]
    grad_mine, grad_other = call(
        bind(grads_kernel, p),
        [((2, p.nyl, p.part_w, LANES), BF), ((p.nyl, p.part_w, 2 * LANES), BF)],
        (rows_x, d_own, d_sib),
        "grads",
    )
    grad_got = exchange(grad_other)
    (share,) = call(
        bind(combine_kernel, p), [((p.nb, p.fin, LANES), BF)], (returned, ranks), "combine"
    )
    last = all_to_all(share, COL)
    grad_mine, grad_got = lax.optimization_barrier((grad_mine, grad_got, share))[:2]
    grad_g, grad_u = call(
        bind(assemble_kernel, p),
        [(shape, BF), (shape, BF)],
        (grad_mine, grad_got),
        "assemble",
    )
    (grad_tokens,) = call(
        bind(finish_kernel, p), [((p.tok, p.part_w), BF)], (last,), "finish"
    )
    out = (1, p.nyl * p.nc * p.part_w, LANES)
    return grad_tokens, grad_g.reshape(out), grad_u.reshape(out)


def solution(mesh):
    sizes = axis_sizes(mesh.shape["expert"], mesh.shape["tensor"])
    inner = Mesh(mesh.devices.reshape(sizes), AXES)
    ex, te = AXES[:3], AXES[3:]
    placed = (
        P(ex, te),
        P(ex, te),
        P(ex, None),
        P(ex, None),
        P(ex, None, te),
        P(ex, None, te),
        P(ex, te, None),
    )
    return jax.shard_map(
        functools.partial(body, sizes),
        mesh=inner,
        in_specs=placed,
        out_specs=(P(ex, te), P(ex, None, te), P(ex, None, te)),
        check_vma=False,
    )
```

```python
import functools

import jax
import jax.numpy as jnp
from jax import lax
from jax.experimental import pallas as pl
from jax.experimental.pallas import tpu as pltpu
from jax.sharding import Mesh, PartitionSpec as P

BF = jnp.bfloat16
F32 = jnp.float32
AXES = ("x", "yh", "z", "yl", "core")
LANES = 128
HALF = 64
VMEM_LIMIT = 24 * 1024 * 1024


def axis_sizes(experts, tensor):
    if (experts, tensor) == (64, 8):
        return (4, 2, 8, 4, 2)
    assert experts % 2 == 0 and tensor == experts
    return (2, 1, experts // 2, tensor // 2, 2)


class Plan:
    def __init__(self, sizes, tok_rows, picks, part_w):
        self.nx, self.nyh, self.nz, self.nyl, self.nc = sizes
        self.tok, self.picks, self.part_w = tok_rows, picks, part_w
        experts = self.nx * self.nyh * self.nz
        self.cap = 3 * tok_rows * picks // (2 * experts)
        self.nb = self.nyh * self.nyl
        assert self.nb == self.nz
        self.nq = self.nx * self.nb
        self.full = part_w // LANES
        assert part_w == self.full * LANES + HALF
        self.groups = 2 * self.full + 1
        self.lanes = self.nb * tok_rows
        self.c = self.nyh * self.cap
        self.grp = self.nb * self.cap
        self.gate_rows = max(8, -(-self.c // 8) * 8, self.nz)
        self.rows = self.nq * self.c
        self.msg = self.groups * self.grp + self.gate_rows
        self.ntail = self.nyl // 2
        self.ret = (self.full + 1) * self.grp
        self.half_d = self.nyl * part_w
        self.pre = self.groups * tok_rows + 2 * picks
        self.fin = (self.full + 1) * tok_rows

    def device(self, x, yh, z, yl, core):
        return (((x * self.nyh + yh) * self.nz + z) * self.nyl + yl) * self.nc + core

    def column_groups(self):
        xs, yhs, zs, yls = map(range, (self.nx, self.nyh, self.nz, self.nyl))
        first = [[self.device(x, h, z, l, 0) for h in yhs for l in yls] for x in xs for z in zs]
        second = [
            [self.device(x, h, z, l, 1) for z in zs] for x in xs for h in yhs for l in yls
        ]
        return first + second

    def plane_groups(self):
        xs, yhs, zs, yls = map(range, (self.nx, self.nyh, self.nz, self.nyl))
        first = [[self.device(x, h, z, l, 0) for x in xs for z in zs] for h in yhs for l in yls]
        second = [[self.device(x, h, z, l, 1) for x in xs for h in yhs for l in yls] for z in zs]
        return first + second


def iota(shape, dim):
    return lax.broadcasted_iota(jnp.int32, shape, dim)


def call(kernel, outs, args, name, scratch=(), flops=0, spaces=None):
    vm = pl.BlockSpec(memory_space=pltpu.VMEM)
    spaces = spaces or {}
    size = sum(a.size * a.dtype.itemsize for a in args) + sum(
        jnp.dtype(o[1]).itemsize * functools.reduce(lambda a, b: a * b, o[0]) for o in outs
    )
    shapes = [jax.ShapeDtypeStruct(s, d) for s, d in outs]
    return pl.pallas_call(
        kernel,
        out_shape=shapes,
        in_specs=[spaces.get(k, vm) for k in range(len(args))],
        out_specs=[vm] * len(outs),
        scratch_shapes=list(scratch),
        compiler_params=pltpu.CompilerParams(vmem_limit_bytes=VMEM_LIMIT),
        cost_estimate=pl.CostEstimate(flops=flops, bytes_accessed=size, transcendentals=0),
        name=name,
    )(*args)


def pack_kernel(p, x_ref, dy_ref, route_ref, gate_ref, out_ref):
    in_y = lax.axis_index("yh") * p.nyl + lax.axis_index("yl")
    block = jnp.where(lax.axis_index("core") == 0, in_y, lax.axis_index("z"))
    top = p.full * LANES
    low = (iota((HALF, LANES), 1) == iota((HALF, LANES), 0)).astype(BF)
    high = (iota((HALF, LANES), 1) == iota((HALF, LANES), 0) + HALF).astype(BF)
    mixed = jnp.dot(x_ref[:, top:], low, preferred_element_type=F32) + jnp.dot(
        dy_ref[:, top:], high, preferred_element_type=F32
    )
    lanes = (iota((p.tok, LANES), 1) == iota((p.tok, LANES), 0) + block * p.tok).astype(BF)
    meta = jnp.concatenate(
        [route_ref[...].astype(F32), gate_ref[...].astype(F32)], axis=0
    ).astype(BF)
    placed = jnp.dot(meta, lanes, preferred_element_type=F32).astype(BF)
    t = p.tok
    for b in range(p.nb):
        for j in range(p.full):
            out_ref[b, j * t : (j + 1) * t, :] = x_ref[:, j * LANES : (j + 1) * LANES]
            k = p.full + 1 + j
            out_ref[b, k * t : (k + 1) * t, :] = dy_ref[:, j * LANES : (j + 1) * LANES]
        out_ref[b, p.full * t : (p.full + 1) * t, :] = mixed.astype(BF)
        out_ref[b, p.groups * t :, :] = placed


def slot_target(p, first):
    r = iota((p.grp, p.lanes), 0)
    b = iota((p.grp, p.lanes), 1) // p.tok
    c = r % p.c
    in_y = jnp.where((r // p.c == b % p.nyl) & (c // p.cap == b // p.nyl), c % p.cap, -2)
    in_z = jnp.where(r % p.nz == b, r // p.nz, -2)
    return jnp.where(first, in_y, in_z).astype(F32)


def gate_target(p, first, rank):
    r = iota((p.gate_rows, p.lanes), 0)
    b = iota((p.gate_rows, p.lanes), 1) // p.tok
    in_y = (r < p.c) & (r % p.cap == rank) & (r // p.cap == b // p.nyl) & (b % p.nyl == 0)
    in_y = jnp.where(in_y, rank, -2)
    in_z = jnp.where(r == b, rank, -2)
    return jnp.where(first, in_y, in_z).astype(F32)


def one_hot(p, ranks, target):
    eq = ranks[:, None, :] == target[None, :, :]
    return jnp.where(eq, 1.0, 0.0).astype(F32).reshape(-1, p.lanes).astype(BF)


def dispatch_kernel(p, in_ref, out_ref, rank_ref):
    first = lax.axis_index("core") == 0
    yh, z = lax.axis_index("yh"), lax.axis_index("z")
    t = p.tok
    meta = in_ref[0, p.groups * t :, :].astype(F32)
    for b in range(1, p.nb):
        meta = meta + in_ref[b, p.groups * t :, :].astype(F32)
    q = iota((p.nq, p.lanes), 0)
    in_y = ((q // p.nz) * p.nyh + yh) * p.nz + q % p.nz
    in_z = (q // p.nyl) * p.nz + z
    expert = jnp.where(first, in_y, in_z).astype(F32)
    hit = jnp.zeros((p.nq, p.lanes), F32)
    gate = jnp.zeros((p.nq, p.lanes), F32)
    for k in range(p.picks):
        same = meta[k : k + 1, : p.lanes] == expert
        hit = hit + jnp.where(same, 1.0, 0.0)
        gate = gate + jnp.where(same, meta[p.picks + k : p.picks + k + 1, : p.lanes], 0.0)
    a, b = iota((p.lanes, p.lanes), 0), iota((p.lanes, p.lanes), 1)
    before = jnp.where((a < b) & (a // t == b // t), 1.0, 0.0).astype(BF)
    rank = jnp.dot(hit.astype(BF), before, preferred_element_type=F32)
    ranks = jnp.where(hit > 0.5, rank, -1.0)
    rank_ref[...] = ranks
    pick = one_hot(p, ranks, slot_target(p, first))
    for g in range(p.groups):
        feats = in_ref[:, g * t : (g + 1) * t, :].reshape(p.lanes, LANES)
        rows = jnp.dot(pick, feats, preferred_element_type=F32)
        out_ref[:, g * p.grp : (g + 1) * p.grp, :] = rows.astype(BF).reshape(p.nq, p.grp, LANES)
    spread = jnp.zeros((p.nq * p.gate_rows, LANES), F32)
    for c in range(p.cap):
        eq = ranks[:, None, :] == gate_target(p, first, c)[None, :, :]
        gates = jnp.where(eq, jnp.broadcast_to(gate[:, None, :], eq.shape), 0.0)
        gates = gates.reshape(p.nq * p.gate_rows, p.lanes).astype(BF)
        here = jnp.where(first, c, iota((p.lanes, LANES), 1)) == c
        lanes = jnp.where(here, 1.0, 0.0).astype(BF)
        spread = spread + jnp.dot(gates, lanes, preferred_element_type=F32)
    out_ref[:, p.groups * p.grp :, :] = spread.astype(BF).reshape(p.nq, p.gate_rows, LANES)


def project_kernel(p, in_ref, wgu_ref, wd_hbm, x_ref, own_ref, sib_ref, gate_ref, flat, dy, wd, sem):
    fetch = pltpu.make_async_copy(wd_hbm, wd, sem)
    fetch.start()
    first = lax.axis_index("core") == 0
    for s in range(p.nq):
        flat[s * p.msg : (s + 1) * p.msg, :] = in_ref[s].astype(F32)
    gate_at = p.groups * p.grp

    def piece_in_y(group, yl):
        row = group * p.grp + yl * p.c
        return jnp.concatenate(
            [flat[pl.ds(row + c, p.nq, stride=p.msg), :] for c in range(p.c)], axis=0
        )

    def blocks():
        for yh in range(p.nyh):
            for c in range(p.cap):
                for x in range(p.nx):
                    yield c, (x * p.nyh + yh) * p.nyl

    def piece_in_z(group, yl):
        rows = [(s + yl) * p.msg + group * p.grp + c * p.nz for c, s in blocks()]
        return jnp.concatenate([flat[r : r + p.nz, :] for r in rows], axis=0)

    def gates_in_y():
        return jnp.concatenate(
            [flat[pl.ds(gate_at + c, p.nq, stride=p.msg), :] for c in range(p.c)], axis=0
        )

    def gates_in_z():
        out = []
        for c, s in blocks():
            row = s * p.msg + gate_at
            out.append(jnp.broadcast_to(flat[row : row + p.nz, c : c + 1], (p.nz, LANES)))
        return jnp.concatenate(out, axis=0)

    left = iota((p.rows, LANES), 1) < HALF

    def arrange(piece, gates):
        for j in range(p.full):
            for yl in range(p.nyl):
                at = (j * p.nyl + yl) * LANES
                x_ref[:, at : at + LANES] = piece(j, yl).astype(BF)
                dy[:, at : at + LANES] = piece(p.full + 1 + j, yl).astype(BF)
        for u in range(p.ntail):
            at = (p.full * p.nyl + u) * LANES
            a = piece(p.full, 2 * u)
            b = piece(p.full, 2 * u + 1)
            x_ref[:, at : at + LANES] = jnp.where(left, a, pltpu.roll(b, HALF, 1)).astype(BF)
            dy[:, at : at + LANES] = jnp.where(left, pltpu.roll(a, HALF, 1), b).astype(BF)
        gate_ref[...] = gates()

    @pl.when(first)
    def _():
        arrange(piece_in_y, gates_in_y)

    @pl.when(jnp.logical_not(first))
    def _():
        arrange(piece_in_z, gates_in_z)

    pre = jnp.dot(x_ref[...], wgu_ref[...], preferred_element_type=F32)
    fetch.wait()
    back = jnp.dot(dy[...], wd[...], preferred_element_type=F32)
    two = 2 * LANES
    own_ref[:, :two] = pre[:, :two]
    sib_ref[:, :two] = pre[:, two:]
    own_ref[:, two:] = back[:, :LANES]
    sib_ref[:, two:] = back[:, LANES:]


def act_kernel(own_ref, got_ref, gate_ref, d_ref):
    pre_gate = own_ref[:, :LANES] + got_ref[:, :LANES]
    pre_up = own_ref[:, LANES : 2 * LANES] + got_ref[:, LANES : 2 * LANES]
    back = own_ref[:, 2 * LANES :] + got_ref[:, 2 * LANES :]
    sig = 1.0 / (1.0 + jnp.exp(-pre_gate))
    scaled = gate_ref[...] * back
    d_ref[:, :LANES] = (scaled * pre_up * sig * (1.0 + pre_gate * (1.0 - sig))).astype(BF)
    d_ref[:, LANES:] = (scaled * pre_gate * sig).astype(BF)


def back_kernel(p, own_ref, sib_ref, wgu_ref, out_ref, flat):
    two = 2 * LANES
    nt = (((1,), (1,)), ((), ()))
    tail = p.full * p.grp
    chunks = p.full * p.nyl

    def part(k):
        at = k * LANES
        return lax.dot_general(
            own_ref[...], wgu_ref[at : at + LANES, :two], nt, preferred_element_type=F32
        ) + lax.dot_general(
            sib_ref[...], wgu_ref[at : at + LANES, two:], nt, preferred_element_type=F32
        )

    def put_in_y(k, value):
        base = k * p.c if k < chunks else tail + (k - chunks) * p.c
        for c in range(p.c):
            flat[pl.ds(base + c, p.nq, stride=p.ret), :] = value[c * p.nq : (c + 1) * p.nq, :]

    def put_in_z(k, value):
        if k < chunks:
            spots = [(k // p.nyl * p.grp, k % p.nyl)]
        else:
            spots = [(tail, 2 * (k - chunks) + h) for h in range(2)]
        for base, yl in spots:
            for i in range(p.rows // p.nz):
                yh, c, x = i // (p.cap * p.nx), i // p.nx % p.cap, i % p.nx
                row = ((x * p.nyh + yh) * p.nyl + yl) * p.ret + base + c * p.nz
                flat[row : row + p.nz, :] = value[i * p.nz : (i + 1) * p.nz, :]

    first = lax.axis_index("core") == 0

    @pl.when(first)
    def _():
        for r in range(tail + p.ntail * p.c, p.ret):
            flat[pl.ds(r, p.nq, stride=p.ret), :] = jnp.zeros((p.nq, LANES), F32)
        for k in range(chunks + p.ntail):
            put_in_y(k, part(k))

    @pl.when(jnp.logical_not(first))
    def _():
        for k in range(chunks + p.ntail):
            put_in_z(k, part(k))

    for s in range(p.nq):
        out_ref[s] = flat[s * p.ret : (s + 1) * p.ret, :].astype(BF)


def combine_kernel(p, in_ref, rank_ref, out_ref):
    t = p.tok
    tn = (((0,), (0,)), ((), ()))
    first = lax.axis_index("core") == 0
    pick = one_hot(p, rank_ref[...], slot_target(p, first))

    def total(g):
        rows = in_ref[:, g * p.grp : (g + 1) * p.grp, :].reshape(p.nq * p.grp, LANES)
        return lax.dot_general(pick, rows, tn, preferred_element_type=F32)

    for g in range(p.full):
        out_ref[:, g * t : (g + 1) * t, :] = total(g).astype(BF).reshape(p.nb, t, LANES)
    last = total(p.full)
    for b in range(p.nb):
        src = (b // p.nyl) * p.nyl + (b % p.nyl) // 2
        value = jnp.where(first, last[src * t : (src + 1) * t, :], last[b * t : (b + 1) * t, :])
        out_ref[b, p.full * t :, :] = value.astype(BF)


def finish_kernel(p, in_ref, out_ref):
    odd = lax.axis_index("yl") % 2
    total = in_ref[0].astype(F32)
    for b in range(1, p.nb):
        total = total + in_ref[b].astype(F32)
    t = p.tok
    for j in range(p.full):
        out_ref[:, j * LANES : (j + 1) * LANES] = total[j * t : (j + 1) * t, :].astype(BF)
    tail = total[p.full * t :, :]
    tail = jnp.where(odd == 1, pltpu.roll(tail, HALF, 1), tail)
    out_ref[:, p.full * LANES :] = tail[:, :HALF].astype(BF)


def grads_kernel(p, x_ref, own_ref, sib_ref, mine_ref, other_ref):
    tn = (((0,), (0,)), ((), ()))

    def put(yl, at, size, src, got, k):
        mine_ref[k, yl, at : at + size, :] = got[src : src + size, k * LANES : (k + 1) * LANES]

    def put_other(yl, at, size, src, got):
        other_ref[yl, at : at + size, :] = got[src : src + size, :]

    for k in range(p.full * p.nyl + p.ntail):
        x = x_ref[:, k * LANES : (k + 1) * LANES]
        mine = lax.dot_general(x, own_ref[...], tn, preferred_element_type=F32).astype(BF)
        other = lax.dot_general(x, sib_ref[...], tn, preferred_element_type=F32).astype(BF)
        if k < p.full * p.nyl:
            spots = [(k % p.nyl, (k // p.nyl) * LANES, LANES, 0)]
        else:
            u = k - p.full * p.nyl
            spots = [(2 * u + h, p.full * LANES, HALF, h * HALF) for h in range(2)]
        for spot in spots:
            put(*spot, mine, 0)
            put(*spot, mine, 1)
            put_other(*spot, other)


def assemble_kernel(p, mine_ref, got_ref, gate_ref, up_ref):
    core = lax.axis_index("core")
    for yl in range(p.nyl):
        gate_ref[yl, core] = mine_ref[0, yl]
        up_ref[yl, core] = mine_ref[1, yl]
        gate_ref[yl, 1 - core] = got_ref[yl, :, :LANES]
        up_ref[yl, 1 - core] = got_ref[yl, :, LANES:]


def lane_tiles(p, w):
    top = p.full * LANES
    n = w.shape[-1]
    tiles = w[:, :top].reshape(p.nyl, p.full, LANES, n).transpose(1, 0, 2, 3).reshape(-1, n)
    return jnp.concatenate([tiles, w[:, top:].reshape(-1, n)], axis=0)


def body(sizes, tokens, grad_out, gate_weights, routing, w_gate, w_up, w_down):
    p = Plan(sizes, *routing.shape, tokens.shape[1])
    swap = [(0, 1), (1, 0)]
    core = lax.axis_index("core")
    bind = functools.partial

    def exchange(v):
        return lax.ppermute(v, "core", swap)

    def all_to_all(v, groups):
        return lax.all_to_all(
            v, AXES, split_axis=0, concat_axis=0, axis_index_groups=groups, tiled=True
        )

    column_groups, plane_groups = p.column_groups(), p.plane_groups()

    (pre,) = call(
        bind(pack_kernel, p),
        [((p.nb, p.pre, LANES), BF)],
        (tokens, grad_out, routing.T, gate_weights.T),
        "pack",
        spaces={k: pl.BlockSpec() for k in range(4)},
    )
    column = all_to_all(pre, column_groups)

    w_gate, w_up, w_down = lax.optimization_barrier((w_gate, w_up, w_down, pre))[:3]
    shape = (p.nyl, p.nc, p.part_w, LANES)
    weights = jnp.stack(
        [w_gate[0].reshape(shape), w_up[0].reshape(shape), w_down[0].T.reshape(shape)]
    )
    mine = lax.dynamic_index_in_dim(weights, core, axis=2, keepdims=False)
    theirs = exchange(lax.dynamic_index_in_dim(weights, 1 - core, axis=2, keepdims=False))
    wgu = lane_tiles(p, jnp.concatenate([mine[0], mine[1], theirs[0], theirs[1]], axis=-1))
    wd = lane_tiles(p, jnp.concatenate([mine[2], theirs[2]], axis=-1))

    sent, ranks = call(
        bind(dispatch_kernel, p),
        [((p.nq, p.msg, LANES), BF), ((p.nq, p.lanes), F32)],
        (column,),
        "dispatch",
    )
    received = all_to_all(sent, plane_groups)
    rows_x, own, sib, gates = call(
        bind(project_kernel, p),
        [
            ((p.rows, p.half_d), BF),
            ((p.rows, 3 * LANES), F32),
            ((p.rows, 3 * LANES), F32),
            ((p.rows, LANES), F32),
        ],
        (received, wgu, wd),
        "project",
        scratch=[
            pltpu.VMEM((p.nq * p.msg, LANES), F32),
            pltpu.VMEM((p.rows, p.half_d), BF),
            pltpu.VMEM((p.half_d, 2 * LANES), BF),
            pltpu.SemaphoreType.DMA,
        ],
        spaces={2: pl.BlockSpec(memory_space=pl.ANY)},
    )
    (d_own,) = call(
        act_kernel, [((p.rows, 2 * LANES), BF)], (own, exchange(sib), gates), "act"
    )
    d_sib = exchange(d_own)
    (back,) = call(
        bind(back_kernel, p),
        [((p.nq, p.ret, LANES), BF)],
        (d_own, d_sib, wgu),
        "back",
        scratch=[pltpu.VMEM((p.nq * p.ret, LANES), F32)],
    )
    returned = all_to_all(back, plane_groups)
    rows_x, d_own, d_sib = lax.optimization_barrier((rows_x, d_own, d_sib, back))[:3]
    grad_mine, grad_other = call(
        bind(grads_kernel, p),
        [((2, p.nyl, p.part_w, LANES), BF), ((p.nyl, p.part_w, 2 * LANES), BF)],
        (rows_x, d_own, d_sib),
        "grads",
    )
    grad_got = exchange(grad_other)
    (share,) = call(
        bind(combine_kernel, p), [((p.nb, p.fin, LANES), BF)], (returned, ranks), "combine"
    )
    last = all_to_all(share, column_groups)
    grad_mine, grad_got = lax.optimization_barrier((grad_mine, grad_got, share))[:2]
    grad_g, grad_u = call(
        bind(assemble_kernel, p),
        [(shape, BF), (shape, BF)],
        (grad_mine, grad_got),
        "assemble",
    )
    (grad_tokens,) = call(
        bind(finish_kernel, p), [((p.tok, p.part_w), BF)], (last,), "finish"
    )
    out = (1, p.nyl * p.nc * p.part_w, LANES)
    return grad_tokens, grad_g.reshape(out), grad_u.reshape(out)


def solution(mesh):
    sizes = axis_sizes(mesh.shape["expert"], mesh.shape["tensor"])
    inner = Mesh(mesh.devices.reshape(sizes), AXES)
    ex, te = AXES[:3], AXES[3:]
    placed = (
        P(ex, te),
        P(ex, te),
        P(ex, None),
        P(ex, None),
        P(ex, None, te),
        P(ex, None, te),
        P(ex, te, None),
    )
    return jax.shard_map(
        functools.partial(body, sizes),
        mesh=inner,
        in_specs=placed,
        out_specs=(P(ex, te), P(ex, None, te), P(ex, None, te)),
        check_vma=False,
    )
```

```python
import functools

import jax
import jax.numpy as jnp
from jax import lax
from jax.experimental import pallas as pl
from jax.experimental.pallas import tpu as pltpu
from jax.sharding import Mesh, PartitionSpec as P

BF = jnp.bfloat16
F32 = jnp.float32
AXES = ("x", "yh", "z", "yl", "core")
LANES = 128
HALF = 64
VMEM_LIMIT = 24 * 1024 * 1024
VMEM_ALL = 67043328
HBM = pl.BlockSpec(memory_space=pltpu.MemorySpace.HBM)


def axis_sizes(experts, tensor):
    if (experts, tensor) == (64, 8):
        return (4, 2, 8, 4, 2)
    assert experts % 2 == 0 and tensor == experts
    return (2, 1, experts // 2, tensor // 2, 2)


class Plan:
    def __init__(self, sizes, tok_rows, picks, part_w):
        self.nx, self.nyh, self.nz, self.nyl, self.nc = sizes
        self.tok, self.picks, self.part_w = tok_rows, picks, part_w
        experts = self.nx * self.nyh * self.nz
        self.cap = 3 * tok_rows * picks // (2 * experts)
        self.nb = self.nyh * self.nyl
        assert self.nb == self.nz
        self.nq = self.nx * self.nb
        self.full = part_w // LANES
        assert part_w == self.full * LANES + HALF
        self.groups = 2 * self.full + 1
        self.lanes = self.nb * tok_rows
        self.c = self.nyh * self.cap
        self.grp = self.nb * self.cap
        self.gate_rows = max(8, -(-self.c // 8) * 8, self.nz)
        self.rows = self.nq * self.c
        self.msg = self.groups * self.grp + self.gate_rows
        self.ntail = self.nyl // 2
        self.ret = (self.full + 1) * self.grp
        self.half_d = self.nyl * part_w
        self.pre = self.groups * tok_rows + 2 * picks
        self.fin = (self.full + 1) * tok_rows

    def device(self, x, yh, z, yl, core):
        return (((x * self.nyh + yh) * self.nz + z) * self.nyl + yl) * self.nc + core

    def column_groups(self):
        xs, yhs, zs, yls = map(range, (self.nx, self.nyh, self.nz, self.nyl))
        first = [[self.device(x, h, z, l, 0) for h in yhs for l in yls] for x in xs for z in zs]
        second = [
            [self.device(x, h, z, l, 1) for z in zs] for x in xs for h in yhs for l in yls
        ]
        return first + second

    def plane_groups(self):
        xs, yhs, zs, yls = map(range, (self.nx, self.nyh, self.nz, self.nyl))
        first = [[self.device(x, h, z, l, 0) for x in xs for z in zs] for h in yhs for l in yls]
        second = [[self.device(x, h, z, l, 1) for x in xs for h in yhs for l in yls] for z in zs]
        return first + second


def iota(shape, dim):
    return lax.broadcasted_iota(jnp.int32, shape, dim)


def call(kernel, outs, args, name, scratch=(), flops=0, spaces=None, limit=VMEM_LIMIT):
    vm = pl.BlockSpec(memory_space=pltpu.VMEM)
    spaces = spaces or {}
    size = sum(a.size * a.dtype.itemsize for a in args) + sum(
        jnp.dtype(o[1]).itemsize * functools.reduce(lambda a, b: a * b, o[0]) for o in outs
    )
    shapes = [jax.ShapeDtypeStruct(s, d) for s, d in outs]
    return pl.pallas_call(
        kernel,
        out_shape=shapes,
        in_specs=[spaces.get(k, vm) for k in range(len(args))],
        out_specs=[vm] * len(outs),
        scratch_shapes=list(scratch),
        compiler_params=pltpu.CompilerParams(vmem_limit_bytes=limit),
        cost_estimate=pl.CostEstimate(flops=flops, bytes_accessed=size, transcendentals=0),
        name=name,
    )(*args)


def pack_kernel(p, *refs):
    out_ref, sems = refs[4], refs[9]
    x_ref, dy_ref, route_ref, gate_ref = refs[5:9]
    fetches = [
        pltpu.make_async_copy(refs[k], refs[5 + k], sems.at[k]) for k in range(4)
    ]
    for fetch in fetches:
        fetch.start()
    for fetch in fetches:
        fetch.wait()
    in_y = lax.axis_index("yh") * p.nyl + lax.axis_index("yl")
    block = jnp.where(lax.axis_index("core") == 0, in_y, lax.axis_index("z"))
    top = p.full * LANES
    low = (iota((HALF, LANES), 1) == iota((HALF, LANES), 0)).astype(BF)
    high = (iota((HALF, LANES), 1) == iota((HALF, LANES), 0) + HALF).astype(BF)
    mixed = jnp.dot(x_ref[:, top:], low, preferred_element_type=F32) + jnp.dot(
        dy_ref[:, top:], high, preferred_element_type=F32
    )
    lanes = (iota((p.tok, LANES), 1) == iota((p.tok, LANES), 0) + block * p.tok).astype(BF)
    meta = jnp.concatenate(
        [route_ref[...].astype(F32), gate_ref[...].astype(F32)], axis=0
    ).astype(BF)
    placed = jnp.dot(meta, lanes, preferred_element_type=F32).astype(BF)
    t = p.tok
    for b in range(p.nb):
        for j in range(p.full):
            out_ref[b, j * t : (j + 1) * t, :] = x_ref[:, j * LANES : (j + 1) * LANES]
            k = p.full + 1 + j
            out_ref[b, k * t : (k + 1) * t, :] = dy_ref[:, j * LANES : (j + 1) * LANES]
        out_ref[b, p.full * t : (p.full + 1) * t, :] = mixed.astype(BF)
        out_ref[b, p.groups * t :, :] = placed


def slot_target(p, first):
    r = iota((p.grp, p.lanes), 0)
    b = iota((p.grp, p.lanes), 1) // p.tok
    c = r % p.c
    in_y = jnp.where((r // p.c == b % p.nyl) & (c // p.cap == b // p.nyl), c % p.cap, -2)
    in_z = jnp.where(r % p.nz == b, r // p.nz, -2)
    return jnp.where(first, in_y, in_z).astype(F32)


def gate_target(p, first, rank):
    r = iota((p.gate_rows, p.lanes), 0)
    b = iota((p.gate_rows, p.lanes), 1) // p.tok
    in_y = (r < p.c) & (r % p.cap == rank) & (r // p.cap == b // p.nyl) & (b % p.nyl == 0)
    in_y = jnp.where(in_y, rank, -2)
    in_z = jnp.where(r == b, rank, -2)
    return jnp.where(first, in_y, in_z).astype(F32)


def one_hot(p, ranks, target):
    eq = ranks[:, None, :] == target[None, :, :]
    return jnp.where(eq, 1.0, 0.0).astype(F32).reshape(-1, p.lanes).astype(BF)


def dispatch_kernel(p, in_ref, out_ref, rank_ref):
    first = lax.axis_index("core") == 0
    yh, z = lax.axis_index("yh"), lax.axis_index("z")
    t = p.tok
    meta = in_ref[0, p.groups * t :, :].astype(F32)
    for b in range(1, p.nb):
        meta = meta + in_ref[b, p.groups * t :, :].astype(F32)
    q = iota((p.nq, p.lanes), 0)
    in_y = ((q // p.nz) * p.nyh + yh) * p.nz + q % p.nz
    in_z = (q // p.nyl) * p.nz + z
    expert = jnp.where(first, in_y, in_z).astype(F32)
    hit = jnp.zeros((p.nq, p.lanes), F32)
    gate = jnp.zeros((p.nq, p.lanes), F32)
    for k in range(p.picks):
        same = meta[k : k + 1, : p.lanes] == expert
        hit = hit + jnp.where(same, 1.0, 0.0)
        gate = gate + jnp.where(same, meta[p.picks + k : p.picks + k + 1, : p.lanes], 0.0)
    a, b = iota((p.lanes, p.lanes), 0), iota((p.lanes, p.lanes), 1)
    before = jnp.where((a < b) & (a // t == b // t), 1.0, 0.0).astype(BF)
    rank = jnp.dot(hit.astype(BF), before, preferred_element_type=F32)
    ranks = jnp.where(hit > 0.5, rank, -1.0)
    rank_ref[...] = ranks
    pick = one_hot(p, ranks, slot_target(p, first))
    for g in range(p.groups):
        feats = in_ref[:, g * t : (g + 1) * t, :].reshape(p.lanes, LANES)
        rows = jnp.dot(pick, feats, preferred_element_type=F32)
        out_ref[:, g * p.grp : (g + 1) * p.grp, :] = rows.astype(BF).reshape(p.nq, p.grp, LANES)
    spread = jnp.zeros((p.nq * p.gate_rows, LANES), F32)
    for c in range(p.cap):
        eq = ranks[:, None, :] == gate_target(p, first, c)[None, :, :]
        gates = jnp.where(eq, jnp.broadcast_to(gate[:, None, :], eq.shape), 0.0)
        gates = gates.reshape(p.nq * p.gate_rows, p.lanes).astype(BF)
        here = jnp.where(first, c, iota((p.lanes, LANES), 1)) == c
        lanes = jnp.where(here, 1.0, 0.0).astype(BF)
        spread = spread + jnp.dot(gates, lanes, preferred_element_type=F32)
    out_ref[:, p.groups * p.grp :, :] = spread.astype(BF).reshape(p.nq, p.gate_rows, LANES)


def project_kernel(p, in_ref, wgu_ref, wd_hbm, x_ref, pre_ref, flat, dy, gate, wd, sem):
    fetch = pltpu.make_async_copy(wd_hbm, wd, sem)
    fetch.start()
    first = lax.axis_index("core") == 0
    gate_at = p.groups * p.grp

    def piece_in_y(group, yl):
        row = group * p.grp + yl * p.c
        return jnp.concatenate(
            [flat[pl.ds(row + c, p.nq, stride=p.msg), :] for c in range(p.c)], axis=0
        )

    def blocks():
        for yh in range(p.nyh):
            for c in range(p.cap):
                for x in range(p.nx):
                    yield c, (x * p.nyh + yh) * p.nyl

    def piece_in_z(group, yl):
        rows = [(s + yl) * p.msg + group * p.grp + c * p.nz for c, s in blocks()]
        return jnp.concatenate([flat[r : r + p.nz, :] for r in rows], axis=0)

    def gates_in_y():
        return jnp.concatenate(
            [flat[pl.ds(gate_at + c, p.nq, stride=p.msg), :] for c in range(p.c)], axis=0
        )

    def gates_in_z():
        out = []
        for c, s in blocks():
            row = s * p.msg + gate_at
            out.append(jnp.broadcast_to(flat[row : row + p.nz, c : c + 1], (p.nz, LANES)))
        return jnp.concatenate(out, axis=0)

    left = iota((p.rows, LANES), 1) < HALF

    def project(piece, gates):
        for s in range(p.nq):
            flat[s * p.msg : (s + 1) * p.msg, :] = in_ref[s].astype(F32)
        for j in range(p.full):
            for yl in range(p.nyl):
                at = (j * p.nyl + yl) * LANES
                x_ref[:, at : at + LANES] = piece(j, yl).astype(BF)
                dy[:, at : at + LANES] = piece(p.full + 1 + j, yl).astype(BF)
        for u in range(p.ntail):
            at = (p.full * p.nyl + u) * LANES
            a = piece(p.full, 2 * u)
            b = piece(p.full, 2 * u + 1)
            x_ref[:, at : at + LANES] = jnp.where(left, a, pltpu.roll(b, HALF, 1)).astype(BF)
            dy[:, at : at + LANES] = jnp.where(left, pltpu.roll(a, HALF, 1), b).astype(BF)
        gate[...] = gates()
        pre = jnp.dot(x_ref[...], wgu_ref[...], preferred_element_type=F32)
        fetch.wait()
        back = jnp.dot(dy[...], wd[...], preferred_element_type=F32)
        two, three = 2 * LANES, 3 * LANES
        pre_ref[:, :two] = pre[:, :two]
        pre_ref[:, two:three] = gate[...] * back[:, :LANES]
        pre_ref[:, three : three + two] = pre[:, two:]
        pre_ref[:, three + two :] = gate[...] * back[:, LANES:]

    @pl.when(first)
    def _():
        project(piece_in_y, gates_in_y)

    @pl.when(jnp.logical_not(first))
    def _():
        project(piece_in_z, gates_in_z)


def back_kernel(p, pre_ref, got_ref, wgu_ref, out_ref, d_ref, flat):
    two, three = 2 * LANES, 3 * LANES
    nt = (((1,), (1,)), ((), ()))
    tail = p.full * p.grp
    chunks = p.full * p.nyl
    for k in range(2):
        mine, theirs = k * three, (1 - k) * three

        def whole(at):
            own = pre_ref[:, mine + at : mine + at + LANES]
            return own + got_ref[:, theirs + at : theirs + at + LANES]

        pre_gate, pre_up, scaled = whole(0), whole(LANES), whole(two)
        sig = 1.0 / (1.0 + jnp.exp(-pre_gate))
        d_gate = scaled * pre_up * sig * (1.0 + pre_gate * (1.0 - sig))
        d_ref[:, k * two : k * two + LANES] = d_gate.astype(BF)
        d_ref[:, k * two + LANES : (k + 1) * two] = (scaled * pre_gate * sig).astype(BF)

    def part(k):
        at = k * LANES
        return lax.dot_general(
            d_ref[...], wgu_ref[at : at + LANES, :], nt, preferred_element_type=F32
        )

    def put_in_y(k, value):
        base = k * p.c if k < chunks else tail + (k - chunks) * p.c
        for c in range(p.c):
            flat[pl.ds(base + c, p.nq, stride=p.ret), :] = value[c * p.nq : (c + 1) * p.nq, :]

    def put_in_z(k, value):
        if k < chunks:
            spots = [(k // p.nyl * p.grp, k % p.nyl)]
        else:
            spots = [(tail, 2 * (k - chunks) + h) for h in range(2)]
        for base, yl in spots:
            for i in range(p.rows // p.nz):
                yh, c, x = i // (p.cap * p.nx), i // p.nx % p.cap, i % p.nx
                row = ((x * p.nyh + yh) * p.nyl + yl) * p.ret + base + c * p.nz
                flat[row : row + p.nz, :] = value[i * p.nz : (i + 1) * p.nz, :]

    def store():
        for s in range(p.nq):
            out_ref[s] = flat[s * p.ret : (s + 1) * p.ret, :].astype(BF)

    first = lax.axis_index("core") == 0

    @pl.when(first)
    def _():
        for r in range(tail + p.ntail * p.c, p.ret):
            flat[pl.ds(r, p.nq, stride=p.ret), :] = jnp.zeros((p.nq, LANES), F32)
        for k in range(chunks + p.ntail):
            put_in_y(k, part(k))
        store()

    @pl.when(jnp.logical_not(first))
    def _():
        for k in range(chunks + p.ntail):
            put_in_z(k, part(k))
        store()


def combine_kernel(p, in_ref, rank_ref, out_ref):
    t = p.tok
    tn = (((0,), (0,)), ((), ()))
    first = lax.axis_index("core") == 0
    pick = one_hot(p, rank_ref[...], slot_target(p, first))

    def total(g):
        rows = in_ref[:, g * p.grp : (g + 1) * p.grp, :].reshape(p.nq * p.grp, LANES)
        return lax.dot_general(pick, rows, tn, preferred_element_type=F32)

    for g in range(p.full):
        out_ref[:, g * t : (g + 1) * t, :] = total(g).astype(BF).reshape(p.nb, t, LANES)
    last = total(p.full)
    for b in range(p.nb):
        src = (b // p.nyl) * p.nyl + (b % p.nyl) // 2
        value = jnp.where(first, last[src * t : (src + 1) * t, :], last[b * t : (b + 1) * t, :])
        out_ref[b, p.full * t :, :] = value.astype(BF)


def finish_kernel(p, in_ref, out_ref):
    odd = lax.axis_index("yl") % 2
    total = in_ref[0].astype(F32)
    for b in range(1, p.nb):
        total = total + in_ref[b].astype(F32)
    t = p.tok
    for j in range(p.full):
        out_ref[:, j * LANES : (j + 1) * LANES] = total[j * t : (j + 1) * t, :].astype(BF)
    tail = total[p.full * t :, :]
    tail = jnp.where(odd == 1, pltpu.roll(tail, HALF, 1), tail)
    out_ref[:, p.full * LANES :] = tail[:, :HALF].astype(BF)


def grads_kernel(p, x_ref, d_ref, mine_ref, other_ref):
    tn = (((0,), (0,)), ((), ()))

    def put(yl, at, size, src, got, k):
        mine_ref[k, yl, at : at + size, :] = got[src : src + size, k * LANES : (k + 1) * LANES]

    def put_other(yl, at, size, src, got):
        other_ref[yl, at : at + size, :] = got[src : src + size, :]

    for k in range(p.full * p.nyl + p.ntail):
        x = x_ref[:, k * LANES : (k + 1) * LANES]
        both = lax.dot_general(x, d_ref[...], tn, preferred_element_type=F32).astype(BF)
        mine, other = both[:, : 2 * LANES], both[:, 2 * LANES :]
        if k < p.full * p.nyl:
            spots = [(k % p.nyl, (k // p.nyl) * LANES, LANES, 0)]
        else:
            u = k - p.full * p.nyl
            spots = [(2 * u + h, p.full * LANES, HALF, h * HALF) for h in range(2)]
        for spot in spots:
            put(*spot, mine, 0)
            put(*spot, mine, 1)
            put_other(*spot, other)


def assemble_kernel(p, mine_ref, got_ref, gate_ref, up_ref):
    core = lax.axis_index("core")
    for yl in range(p.nyl):
        gate_ref[yl, core] = mine_ref[0, yl]
        up_ref[yl, core] = mine_ref[1, yl]
        gate_ref[yl, 1 - core] = got_ref[yl, :, :LANES]
        up_ref[yl, 1 - core] = got_ref[yl, :, LANES:]


def lane_tiles(p, w):
    top = p.full * LANES
    n = w.shape[-1]
    tiles = w[:, :top].reshape(p.nyl, p.full, LANES, n).transpose(1, 0, 2, 3).reshape(-1, n)
    return jnp.concatenate([tiles, w[:, top:].reshape(-1, n)], axis=0)


def body(sizes, tokens, grad_out, gate_weights, routing, w_gate, w_up, w_down):
    p = Plan(sizes, *routing.shape, tokens.shape[1])
    swap = [(0, 1), (1, 0)]
    core = lax.axis_index("core")
    bind = functools.partial

    def exchange(v):
        return lax.ppermute(v, "core", swap)

    def all_to_all(v, groups):
        return lax.all_to_all(
            v, AXES, split_axis=0, concat_axis=0, axis_index_groups=groups, tiled=True
        )

    column_groups, plane_groups = p.column_groups(), p.plane_groups()

    (pre,) = call(
        bind(pack_kernel, p),
        [((p.nb, p.pre, LANES), BF)],
        (tokens, grad_out, routing.T, gate_weights.T),
        "pack",
        scratch=[
            pltpu.VMEM(tokens.shape, BF),
            pltpu.VMEM(grad_out.shape, BF),
            pltpu.VMEM(routing.shape[::-1], routing.dtype),
            pltpu.VMEM(gate_weights.shape[::-1], BF),
            pltpu.SemaphoreType.DMA((4,)),
        ],
        spaces={k: HBM for k in range(4)},
        limit=VMEM_ALL,
    )
    column = all_to_all(pre, column_groups)

    w_gate, w_up, w_down = lax.optimization_barrier((w_gate, w_up, w_down, pre))[:3]
    shape = (p.nyl, p.nc, p.part_w, LANES)
    weights = jnp.stack(
        [w_gate[0].reshape(shape), w_up[0].reshape(shape), w_down[0].T.reshape(shape)]
    )
    mine = lax.dynamic_index_in_dim(weights, core, axis=2, keepdims=False)
    theirs = exchange(lax.dynamic_index_in_dim(weights, 1 - core, axis=2, keepdims=False))
    wgu = lane_tiles(p, jnp.concatenate([mine[0], mine[1], theirs[0], theirs[1]], axis=-1))
    wd = lane_tiles(p, jnp.concatenate([mine[2], theirs[2]], axis=-1))

    sent, ranks = call(
        bind(dispatch_kernel, p),
        [((p.nq, p.msg, LANES), BF), ((p.nq, p.lanes), F32)],
        (column,),
        "dispatch",
    )
    received = all_to_all(sent, plane_groups)
    rows_x, partial = call(
        bind(project_kernel, p),
        [
            ((p.rows, p.half_d), BF),
            ((p.rows, 6 * LANES), F32),
        ],
        (received, wgu, wd),
        "project",
        scratch=[
            pltpu.VMEM((p.nq * p.msg, LANES), F32),
            pltpu.VMEM((p.rows, p.half_d), BF),
            pltpu.VMEM((p.rows, LANES), F32),
            pltpu.VMEM((p.half_d, 2 * LANES), BF),
            pltpu.SemaphoreType.DMA,
        ],
        spaces={2: HBM},
    )
    back, d_all = call(
        bind(back_kernel, p),
        [((p.nq, p.ret, LANES), BF), ((p.rows, 4 * LANES), BF)],
        (partial, exchange(partial), wgu),
        "back",
        scratch=[pltpu.VMEM((p.nq * p.ret, LANES), F32)],
    )
    returned = all_to_all(back, plane_groups)
    rows_x, d_all = lax.optimization_barrier((rows_x, d_all, back))[:2]
    grad_mine, grad_other = call(
        bind(grads_kernel, p),
        [((2, p.nyl, p.part_w, LANES), BF), ((p.nyl, p.part_w, 2 * LANES), BF)],
        (rows_x, d_all),
        "grads",
    )
    grad_got = exchange(grad_other)
    (share,) = call(
        bind(combine_kernel, p), [((p.nb, p.fin, LANES), BF)], (returned, ranks), "combine"
    )
    last = all_to_all(share, column_groups)
    grad_mine, grad_got = lax.optimization_barrier((grad_mine, grad_got, share))[:2]
    grad_g, grad_u = call(
        bind(assemble_kernel, p),
        [(shape, BF), (shape, BF)],
        (grad_mine, grad_got),
        "assemble",
    )
    (grad_tokens,) = call(
        bind(finish_kernel, p), [((p.tok, p.part_w), BF)], (last,), "finish"
    )
    out = (1, p.nyl * p.nc * p.part_w, LANES)
    return grad_tokens, grad_g.reshape(out), grad_u.reshape(out)


def solution(mesh):
    sizes = axis_sizes(mesh.shape["expert"], mesh.shape["tensor"])
    inner = Mesh(mesh.devices.reshape(sizes), AXES)
    ex, te = AXES[:3], AXES[3:]
    placed = (
        P(ex, te),
        P(ex, te),
        P(ex, None),
        P(ex, None),
        P(ex, None, te),
        P(ex, None, te),
        P(ex, te, None),
    )
    return jax.shard_map(
        functools.partial(body, sizes),
        mesh=inner,
        in_specs=placed,
        out_specs=(P(ex, te), P(ex, None, te), P(ex, None, te)),
        check_vma=False,
    )
```

```python
import functools

import jax
import jax.numpy as jnp
from jax import lax
from jax.experimental import pallas as pl
from jax.experimental.pallas import tpu as pltpu
from jax.sharding import Mesh, PartitionSpec as P

BF = jnp.bfloat16
F32 = jnp.float32
AXES = ("x", "yh", "z", "yl", "core")
LANES = 128
HALF = 64
VMEM_LIMIT = 16 * 1024 * 1024
STASH_ROWS = 40 * 1024
VMEM_ALL = 67043328
HBM = pl.BlockSpec(memory_space=pltpu.MemorySpace.HBM)


def axis_sizes(experts, tensor):
    if (experts, tensor) == (64, 8):
        return (4, 2, 8, 4, 2)
    assert experts % 2 == 0 and tensor == experts
    return (2, 1, experts // 2, tensor // 2, 2)


def pitch(rows):
    tiles = -(-rows // 8)
    return 8 * (tiles + 1 - tiles % 2)


class Plan:
    def __init__(self, sizes, tok_rows, picks, part_w):
        self.nx, self.nyh, self.nz, self.nyl, self.nc = sizes
        self.tok, self.picks, self.part_w = tok_rows, picks, part_w
        experts = self.nx * self.nyh * self.nz
        self.cap = 3 * tok_rows * picks // (2 * experts)
        self.nb = self.nyh * self.nyl
        assert self.nb == self.nz
        self.nq = self.nx * self.nb
        self.full = part_w // LANES
        assert part_w == self.full * LANES + HALF
        self.groups = 2 * self.full + 1
        self.lanes = self.nb * tok_rows
        self.c = self.nyh * self.cap
        self.grp = self.nb * self.cap
        self.rows = self.nq * self.c
        self.msg = self.groups * self.grp
        self.pitch = pitch(self.msg)
        self.ntail = self.nyl // 2
        self.pairs = (self.cap + 1) // 2
        self.tail = -(-max(self.ntail * self.c, self.pairs * self.nz) // 8) * 8
        self.ret = self.full * self.grp + self.tail
        self.ret_pitch = pitch(self.ret)
        self.half_d = self.nyl * part_w
        self.pre = self.groups * tok_rows + 2 * picks
        self.fin = (self.full + 1) * tok_rows

    def device(self, x, yh, z, yl, core):
        return (((x * self.nyh + yh) * self.nz + z) * self.nyl + yl) * self.nc + core

    def column_groups(self):
        xs, yhs, zs, yls = map(range, (self.nx, self.nyh, self.nz, self.nyl))
        first = [[self.device(x, h, z, l, 0) for h in yhs for l in yls] for x in xs for z in zs]
        second = [
            [self.device(x, h, z, l, 1) for z in zs] for x in xs for h in yhs for l in yls
        ]
        return first + second

    def plane_groups(self):
        xs, yhs, zs, yls = map(range, (self.nx, self.nyh, self.nz, self.nyl))
        first = [[self.device(x, h, z, l, 0) for x in xs for z in zs] for h in yhs for l in yls]
        second = [[self.device(x, h, z, l, 1) for x in xs for h in yhs for l in yls] for z in zs]
        return first + second


def iota(shape, dim):
    return lax.broadcasted_iota(jnp.int32, shape, dim)


def call(kernel, outs, args, scratch=(), flops=0, spaces=None, limit=VMEM_LIMIT, out_spec=None):
    vm = pl.BlockSpec(memory_space=pltpu.VMEM)
    spaces = spaces or {}
    size = sum(a.size * a.dtype.itemsize for a in args) + sum(
        jnp.dtype(o[1]).itemsize * functools.reduce(lambda a, b: a * b, o[0]) for o in outs
    )
    shapes = [jax.ShapeDtypeStruct(s, d) for s, d in outs]
    return pl.pallas_call(
        kernel,
        out_shape=shapes,
        in_specs=[spaces.get(k, vm) for k in range(len(args))],
        out_specs=[out_spec or vm] * len(outs),
        scratch_shapes=list(scratch),
        compiler_params=pltpu.CompilerParams(vmem_limit_bytes=limit),
        cost_estimate=pl.CostEstimate(flops=flops, bytes_accessed=size, transcendentals=0),
    )(*args)


def pack_kernel(p, *refs):
    out_ref, sems = refs[4], refs[9]
    x_ref, dy_ref, route_ref, gate_ref = refs[5:9]
    fetches = [
        pltpu.make_async_copy(refs[k], refs[5 + k], sems.at[k]) for k in range(4)
    ]
    for fetch in fetches:
        fetch.start()
    for fetch in fetches:
        fetch.wait()
    in_y = lax.axis_index("yh") * p.nyl + lax.axis_index("yl")
    block = jnp.where(lax.axis_index("core") == 0, in_y, lax.axis_index("z"))
    top = p.full * LANES
    low = (iota((HALF, LANES), 1) == iota((HALF, LANES), 0)).astype(BF)
    high = (iota((HALF, LANES), 1) == iota((HALF, LANES), 0) + HALF).astype(BF)
    mixed = jnp.dot(x_ref[:, top:], low, preferred_element_type=F32) + jnp.dot(
        dy_ref[:, top:], high, preferred_element_type=F32
    )
    lanes = (iota((p.tok, LANES), 1) == iota((p.tok, LANES), 0) + block * p.tok).astype(BF)
    meta = jnp.concatenate(
        [route_ref[...].astype(F32), gate_ref[...].astype(F32)], axis=0
    ).astype(BF)
    placed = jnp.dot(meta, lanes, preferred_element_type=F32).astype(BF)
    t = p.tok
    for b in range(p.nb):
        for j in range(p.full):
            out_ref[b, j * t : (j + 1) * t, :] = x_ref[:, j * LANES : (j + 1) * LANES]
            k = p.full + 1 + j
            out_ref[b, k * t : (k + 1) * t, :] = dy_ref[:, j * LANES : (j + 1) * LANES]
        out_ref[b, p.full * t : (p.full + 1) * t, :] = mixed.astype(BF)
        out_ref[b, p.groups * t :, :] = placed


def slot_target(p, first):
    r = iota((p.grp, p.lanes), 0)
    b = iota((p.grp, p.lanes), 1) // p.tok
    c = r % p.c
    in_y = jnp.where((r // p.c == b % p.nyl) & (c // p.cap == b // p.nyl), c % p.cap, -2)
    in_z = jnp.where(r % p.nz == b, r // p.nz, -2)
    return jnp.where(first, in_y, in_z).astype(F32)


def one_hot(p, ranks, target, weight=1.0):
    eq = ranks[:, None, :] == target[None, :, :]
    return jnp.where(eq, weight, 0.0).astype(F32).reshape(-1, p.lanes).astype(BF)


def dispatch_kernel(p, in_ref, out_ref, rank_ref):
    first = lax.axis_index("core") == 0
    yh, z = lax.axis_index("yh"), lax.axis_index("z")
    t = p.tok
    meta = in_ref[0, p.groups * t :, :].astype(F32)
    for b in range(1, p.nb):
        meta = meta + in_ref[b, p.groups * t :, :].astype(F32)
    q = iota((p.nq, p.lanes), 0)
    in_y = ((q // p.nz) * p.nyh + yh) * p.nz + q % p.nz
    in_z = (q // p.nyl) * p.nz + z
    expert = jnp.where(first, in_y, in_z).astype(F32)
    hit = jnp.zeros((p.nq, p.lanes), F32)
    gate = jnp.zeros((p.nq, p.lanes), F32)
    for k in range(p.picks):
        same = meta[k : k + 1, : p.lanes] == expert
        hit = hit + jnp.where(same, 1.0, 0.0)
        gate = gate + jnp.where(same, meta[p.picks + k : p.picks + k + 1, : p.lanes], 0.0)
    a, b = iota((p.lanes, p.lanes), 0), iota((p.lanes, p.lanes), 1)
    before = jnp.where((a < b) & (a // t == b // t), 1.0, 0.0).astype(BF)
    rank = jnp.dot(hit.astype(BF), before, preferred_element_type=F32)
    ranks = jnp.where(hit > 0.5, rank, -1.0)
    rank_ref[...] = ranks
    target = slot_target(p, first)
    pick = one_hot(p, ranks, target)
    gate = jnp.broadcast_to(gate[:, None, :], (p.nq, p.grp, p.lanes))
    scaled = one_hot(p, ranks, target, gate)
    left = iota((p.nq * p.grp, LANES), 1) < HALF
    for g in range(p.groups):
        feats = in_ref[:, g * t : (g + 1) * t, :].reshape(p.lanes, LANES)
        rows = jnp.dot(pick if g <= p.full else scaled, feats, preferred_element_type=F32)
        if g == p.full:
            both = jnp.dot(scaled, feats, preferred_element_type=F32)
            rows = jnp.where(left, rows, both)
        out_ref[:, g * p.grp : (g + 1) * p.grp, :] = rows.astype(BF).reshape(p.nq, p.grp, LANES)


def project_kernel(p, in_ref, wgu_ref, wd_hbm, x_ref, pre_ref, flat, dy, wd, sem):
    fetch = pltpu.make_async_copy(wd_hbm.at[: p.half_d], wd, sem)
    fetch.start()
    first = lax.axis_index("core") == 0

    def piece_in_y(group, yl):
        row = group * p.grp + yl * p.c
        return jnp.concatenate(
            [flat[pl.ds(row + c, p.nq, stride=p.pitch), :] for c in range(p.c)], axis=0
        )

    def blocks():
        for yh in range(p.nyh):
            for c in range(p.cap):
                for x in range(p.nx):
                    yield c, (x * p.nyh + yh) * p.nyl

    def piece_in_z(group, yl):
        rows = [(s + yl) * p.pitch + group * p.grp + c * p.nz for c, s in blocks()]
        return jnp.concatenate([flat[r : r + p.nz, :] for r in rows], axis=0)

    left = iota((p.rows, LANES), 1) < HALF

    def project(piece):
        for s in range(p.nq):
            flat[s * p.pitch : s * p.pitch + p.msg, :] = in_ref[s].astype(F32)
        for j in range(p.full):
            for yl in range(p.nyl):
                at = (j * p.nyl + yl) * LANES
                x_ref[:, at : at + LANES] = piece(j, yl).astype(BF)
                dy[:, at : at + LANES] = piece(p.full + 1 + j, yl).astype(BF)
        for u in range(p.ntail):
            at = (p.full * p.nyl + u) * LANES
            a = piece(p.full, 2 * u)
            b = piece(p.full, 2 * u + 1)
            x_ref[:, at : at + LANES] = jnp.where(left, a, pltpu.roll(b, HALF, 1)).astype(BF)
            dy[:, at : at + LANES] = jnp.where(left, pltpu.roll(a, HALF, 1), b).astype(BF)
        pre = jnp.dot(x_ref[...], wgu_ref[...], preferred_element_type=F32)
        fetch.wait()
        back = jnp.dot(dy[...], wd[...], preferred_element_type=F32)
        two, three = 2 * LANES, 3 * LANES
        pre_ref[:, :two] = pre[:, :two]
        pre_ref[:, two:three] = back[:, :LANES]
        pre_ref[:, three : three + two] = pre[:, two:]
        pre_ref[:, three + two :] = back[:, LANES:]

    @pl.when(first)
    def _():
        project(piece_in_y)

    @pl.when(jnp.logical_not(first))
    def _():
        project(piece_in_z)


def stash_kernel(in_ref, out_ref, sem):
    copy = pltpu.make_async_copy(in_ref, out_ref.at[: in_ref.shape[0]], sem)
    copy.start()
    copy.wait()


def back_kernel(p, pre_ref, got_ref, wgu_ref, out_ref, d_ref, flat):
    two, three = 2 * LANES, 3 * LANES
    nt = (((1,), (1,)), ((), ()))
    tail = p.full * p.grp
    chunks = p.full * p.nyl
    left = iota((p.nz, LANES), 1) < HALF
    for k in range(2):
        mine, theirs = k * three, (1 - k) * three

        def whole(at):
            own = pre_ref[:, mine + at : mine + at + LANES]
            return own + got_ref[:, theirs + at : theirs + at + LANES]

        pre_gate, pre_up, scaled = whole(0), whole(LANES), whole(two)
        sig = 1.0 / (1.0 + jnp.exp(-pre_gate))
        d_gate = scaled * pre_up * sig * (1.0 + pre_gate * (1.0 - sig))
        d_ref[:, k * two : k * two + LANES] = d_gate.astype(BF)
        d_ref[:, k * two + LANES : (k + 1) * two] = (scaled * pre_gate * sig).astype(BF)

    def part(k):
        at = k * LANES
        return lax.dot_general(
            d_ref[...], wgu_ref[at : at + LANES, :], nt, preferred_element_type=F32
        )

    def put_in_y(k, value):
        base = k * p.c if k < chunks else tail + (k - chunks) * p.c
        for c in range(p.c):
            flat[pl.ds(base + c, p.nq, stride=p.ret_pitch), :] = value[c * p.nq : (c + 1) * p.nq, :]

    def put_in_z(k, value):
        def block(yh, c, x):
            at = ((yh * p.cap + c) * p.nx + x) * p.nz
            return value[at : at + p.nz, :]

        for yh in range(p.nyh):
            for x in range(p.nx):
                s = (x * p.nyh + yh) * p.nyl
                if k < chunks:
                    for c in range(p.cap):
                        row = (s + k % p.nyl) * p.ret_pitch + k // p.nyl * p.grp + c * p.nz
                        flat[row : row + p.nz, :] = block(yh, c, x)
                    continue
                for c in range(0, p.cap, 2):
                    one = block(yh, c, x)
                    two = block(yh, c + 1, x) if c + 1 < p.cap else one
                    ends = (
                        jnp.where(left, one, pltpu.roll(two, HALF, 1)),
                        jnp.where(left, pltpu.roll(one, HALF, 1), two),
                    )
                    for h in range(2):
                        row = (s + 2 * (k - chunks) + h) * p.ret_pitch + tail + c // 2 * p.nz
                        flat[row : row + p.nz, :] = ends[h]

    def store():
        for s in range(p.nq):
            out_ref[s] = flat[s * p.ret_pitch : s * p.ret_pitch + p.ret, :].astype(BF)

    first = lax.axis_index("core") == 0

    @pl.when(first)
    def _():
        for r in range(tail + p.ntail * p.c, tail + p.tail):
            flat[pl.ds(r, p.nq, stride=p.ret_pitch), :] = jnp.zeros((p.nq, LANES), F32)
        for k in range(chunks + p.ntail):
            put_in_y(k, part(k))
        store()

    @pl.when(jnp.logical_not(first))
    def _():
        for k in range(chunks + p.ntail):
            put_in_z(k, part(k))
        store()


def combine_kernel(p, in_ref, rank_ref, out_ref):
    t = p.tok
    tn = (((0,), (0,)), ((), ()))
    first = lax.axis_index("core") == 0
    pick = one_hot(p, rank_ref[...], slot_target(p, first))

    def total(g):
        rows = in_ref[:, g * p.grp : (g + 1) * p.grp, :].reshape(p.nq * p.grp, LANES)
        return lax.dot_general(pick, rows, tn, preferred_element_type=F32)

    for g in range(p.full):
        out_ref[:, g * t : (g + 1) * t, :] = total(g).astype(BF).reshape(p.nb, t, LANES)
    tail = p.full * p.grp
    pick = pick.reshape(p.nq, p.grp, p.lanes)

    def tail_total(start, stop, at):
        rows = in_ref[:, tail + at : tail + at + stop - start, :].reshape(-1, LANES)
        chosen = pick[:, start:stop, :].reshape(-1, p.lanes)
        return lax.dot_general(chosen, rows, tn, preferred_element_type=F32)

    @pl.when(first)
    def _():
        last = tail_total(0, p.tail, 0)
        for b in range(p.nb):
            src = (b // p.nyl) * p.nyl + (b % p.nyl) // 2
            out_ref[b, p.full * t :, :] = last[src * t : (src + 1) * t, :].astype(BF)

    @pl.when(jnp.logical_not(first))
    def _():
        sides = [None, None]
        for c in range(p.cap):
            part = tail_total(c * p.nz, (c + 1) * p.nz, c // 2 * p.nz)
            sides[c % 2] = part if sides[c % 2] is None else sides[c % 2] + part
        last = sides[0] + pltpu.roll(sides[1], HALF, 1)
        out_ref[:, p.full * t :, :] = last.astype(BF).reshape(p.nb, t, LANES)


def finish_kernel(p, in_ref, out_ref):
    odd = jnp.where(lax.axis_index("core") == 0, lax.axis_index("yl") % 2, 0)
    total = in_ref[0].astype(F32)
    for b in range(1, p.nb):
        total = total + in_ref[b].astype(F32)
    t = p.tok
    for j in range(p.full):
        out_ref[:, j * LANES : (j + 1) * LANES] = total[j * t : (j + 1) * t, :].astype(BF)
    tail = total[p.full * t :, :]
    tail = jnp.where(odd == 1, pltpu.roll(tail, HALF, 1), tail)
    out_ref[:, p.full * LANES :] = tail[:, :HALF].astype(BF)


def grads_kernel(p, x_ref, d_ref, mine_ref, other_ref):
    tn = (((0,), (0,)), ((), ()))

    def put(yl, at, size, src, got, k):
        mine_ref[k, yl, at : at + size, :] = got[src : src + size, k * LANES : (k + 1) * LANES]

    def put_other(yl, at, size, src, got):
        other_ref[yl, at : at + size, :] = got[src : src + size, :]

    for k in range(p.full * p.nyl + p.ntail):
        x = x_ref[:, k * LANES : (k + 1) * LANES]
        both = lax.dot_general(x, d_ref[...], tn, preferred_element_type=F32).astype(BF)
        mine, other = both[:, : 2 * LANES], both[:, 2 * LANES :]
        if k < p.full * p.nyl:
            spots = [(k % p.nyl, (k // p.nyl) * LANES, LANES, 0)]
        else:
            u = k - p.full * p.nyl
            spots = [(2 * u + h, p.full * LANES, HALF, h * HALF) for h in range(2)]
        for spot in spots:
            put(*spot, mine, 0)
            put(*spot, mine, 1)
            put_other(*spot, other)


def assemble_kernel(p, mine_ref, got_ref, gate_ref, up_ref):
    core = lax.axis_index("core")
    for yl in range(p.nyl):
        gate_ref[yl, core] = mine_ref[0, yl]
        up_ref[yl, core] = mine_ref[1, yl]
        gate_ref[yl, 1 - core] = got_ref[yl, :, :LANES]
        up_ref[yl, 1 - core] = got_ref[yl, :, LANES:]


def lane_tiles(p, w):
    top = p.full * LANES
    n = w.shape[-1]
    tiles = w[:, :top].reshape(p.nyl, p.full, LANES, n).transpose(1, 0, 2, 3).reshape(-1, n)
    return jnp.concatenate([tiles, w[:, top:].reshape(-1, n)], axis=0)


def body(sizes, *args):
    return program(sizes, *args)


def program(sizes, tokens, grad_out, gate_weights, routing, w_gate, w_up, w_down):
    p = Plan(sizes, *routing.shape, tokens.shape[1])
    swap = [(0, 1), (1, 0)]
    core = lax.axis_index("core")
    bind = functools.partial

    def exchange(v):
        return lax.ppermute(v, "core", swap)

    def all_to_all(v, groups):
        return lax.all_to_all(
            v, AXES, split_axis=0, concat_axis=0, axis_index_groups=groups, tiled=True
        )

    column_groups, plane_groups = p.column_groups(), p.plane_groups()

    (pre,) = call(
        bind(pack_kernel, p),
        [((p.nb, p.pre, LANES), BF)],
        (tokens, grad_out, routing.T, gate_weights.T),
        scratch=[
            pltpu.VMEM(tokens.shape, BF),
            pltpu.VMEM(grad_out.shape, BF),
            pltpu.VMEM(routing.shape[::-1], routing.dtype),
            pltpu.VMEM(gate_weights.shape[::-1], BF),
            pltpu.SemaphoreType.DMA((4,)),
        ],
        spaces={k: HBM for k in range(4)},
        limit=VMEM_ALL,
    )
    column = all_to_all(pre, column_groups)

    w_gate, w_up, w_down = lax.optimization_barrier((w_gate, w_up, w_down, pre))[:3]
    shape = (p.nyl, p.nc, p.part_w, LANES)
    weights = jnp.stack(
        [w_gate[0].reshape(shape), w_up[0].reshape(shape), w_down[0].T.reshape(shape)]
    )
    mine = lax.dynamic_index_in_dim(weights, core, axis=2, keepdims=False)
    other = lax.dynamic_index_in_dim(weights, 1 - core, axis=2, keepdims=False)
    theirs = exchange(other)
    wgu = lane_tiles(p, jnp.concatenate([mine[0], mine[1], theirs[0], theirs[1]], axis=-1))
    wd = lane_tiles(p, jnp.concatenate([mine[2], theirs[2]], axis=-1))
    (wd,) = call(
        stash_kernel,
        [((STASH_ROWS, 2 * LANES), BF)],
        (wd,),
        scratch=[pltpu.SemaphoreType.DMA],
        out_spec=HBM,
        limit=3 * VMEM_LIMIT,
    )

    sent, ranks = call(
        bind(dispatch_kernel, p), [((p.nq, p.msg, LANES), BF), ((p.nq, p.lanes), F32)], (column,)
    )
    received = all_to_all(sent, plane_groups)
    rows_x, partial = call(
        bind(project_kernel, p),
        [
            ((p.rows, p.half_d), BF),
            ((p.rows, 6 * LANES), F32),
        ],
        (received, wgu, wd),
        scratch=[
            pltpu.VMEM((p.nq * p.pitch, LANES), F32),
            pltpu.VMEM((p.rows, p.half_d), BF),
            pltpu.VMEM((p.half_d, 2 * LANES), BF),
            pltpu.SemaphoreType.DMA,
        ],
        spaces={2: HBM},
        limit=3 * VMEM_LIMIT,
    )
    back, d_all = call(
        bind(back_kernel, p),
        [((p.nq, p.ret, LANES), BF), ((p.rows, 4 * LANES), BF)],
        (partial, exchange(partial), wgu),
        scratch=[pltpu.VMEM((p.nq * p.ret_pitch, LANES), F32)],
    )
    returned = all_to_all(back, plane_groups)
    rows_x, d_all = lax.optimization_barrier((rows_x, d_all, back))[:2]
    grad_mine, grad_other = call(
        bind(grads_kernel, p),
        [((2, p.nyl, p.part_w, LANES), BF), ((p.nyl, p.part_w, 2 * LANES), BF)],
        (rows_x, d_all),
    )
    grad_got = exchange(grad_other)
    (share,) = call(bind(combine_kernel, p), [((p.nb, p.fin, LANES), BF)], (returned, ranks))
    last = all_to_all(share, column_groups)
    grad_mine, grad_got = lax.optimization_barrier((grad_mine, grad_got, share))[:2]
    grad_g, grad_u = call(
        bind(assemble_kernel, p), [(shape, BF), (shape, BF)], (grad_mine, grad_got)
    )
    (grad_tokens,) = call(bind(finish_kernel, p), [((p.tok, p.part_w), BF)], (last,))
    out = (1, p.nyl * p.nc * p.part_w, LANES)
    return grad_tokens, grad_g.reshape(out), grad_u.reshape(out)


def solution(mesh):
    sizes = axis_sizes(mesh.shape["expert"], mesh.shape["tensor"])
    inner = Mesh(mesh.devices.reshape(sizes), AXES)
    ex, te = AXES[:3], AXES[3:]
    placed = (
        P(ex, te),
        P(ex, te),
        P(ex, None),
        P(ex, None),
        P(ex, None, te),
        P(ex, None, te),
        P(ex, te, None),
    )
    return jax.shard_map(
        functools.partial(body, sizes),
        mesh=inner,
        in_specs=placed,
        out_specs=(P(ex, te), P(ex, None, te), P(ex, None, te)),
        check_vma=False,
    )
```

```python
import functools

import jax
import jax.numpy as jnp
from jax import lax
from jax.experimental import pallas as pl
from jax.experimental.pallas import tpu as pltpu
from jax.sharding import Mesh, PartitionSpec as P

BF = jnp.bfloat16
F32 = jnp.float32
AXES = ("x", "yh", "z", "yl", "core")
LANES = 128
HALF = 64
VMEM_LIMIT = 16 * 1024 * 1024
STASH_ROWS = 40 * 1024
VMEM_ALL = 67043328
HBM = pl.BlockSpec(memory_space=pltpu.MemorySpace.HBM)


def axis_sizes(experts, tensor):
    if (experts, tensor) == (64, 8):
        return (4, 2, 8, 4, 2)
    assert experts % 2 == 0 and tensor == experts
    return (2, 1, experts // 2, tensor // 2, 2)


def pitch(rows):
    tiles = -(-rows // 8)
    return 8 * (tiles + 1 - tiles % 2)


class Plan:
    def __init__(self, sizes, tok_rows, picks, part_w):
        self.nx, self.nyh, self.nz, self.nyl, self.nc = sizes
        self.tok, self.picks, self.part_w = tok_rows, picks, part_w
        experts = self.nx * self.nyh * self.nz
        self.cap = 3 * tok_rows * picks // (2 * experts)
        self.nb = self.nyh * self.nyl
        assert self.nb == self.nz
        self.nq = self.nx * self.nb
        self.full = part_w // LANES
        assert part_w == self.full * LANES + HALF
        self.groups = 2 * self.full + 1
        self.lanes = self.nb * tok_rows
        self.c = self.nyh * self.cap
        self.grp = self.nb * self.cap
        self.rows = self.nq * self.c
        self.msg = self.groups * self.grp
        self.pitch = pitch(self.msg)
        self.ntail = self.nyl // 2
        self.pairs = (self.cap + 1) // 2
        self.tail = -(-max(self.ntail * self.c, self.pairs * self.nz) // 8) * 8
        self.ret = self.full * self.grp + self.tail
        self.ret_pitch = pitch(self.ret)
        self.half_d = self.nyl * part_w
        self.pre = self.groups * tok_rows + 2 * picks
        self.fin = (self.full + 1) * tok_rows

    def device(self, x, yh, z, yl, core):
        return (((x * self.nyh + yh) * self.nz + z) * self.nyl + yl) * self.nc + core

    def column_groups(self):
        xs, yhs, zs, yls = map(range, (self.nx, self.nyh, self.nz, self.nyl))
        first = [[self.device(x, h, z, l, 0) for h in yhs for l in yls] for x in xs for z in zs]
        second = [
            [self.device(x, h, z, l, 1) for z in zs] for x in xs for h in yhs for l in yls
        ]
        return first + second

    def plane_groups(self):
        xs, yhs, zs, yls = map(range, (self.nx, self.nyh, self.nz, self.nyl))
        first = [[self.device(x, h, z, l, 0) for x in xs for z in zs] for h in yhs for l in yls]
        second = [[self.device(x, h, z, l, 1) for x in xs for h in yhs for l in yls] for z in zs]
        return first + second


def iota(shape, dim):
    return lax.broadcasted_iota(jnp.int32, shape, dim)


def call(kernel, outs, args, scratch=(), flops=0, spaces=None, limit=VMEM_LIMIT, out_spaces=None):
    vm = pl.BlockSpec(memory_space=pltpu.VMEM)
    spaces = spaces or {}
    size = sum(a.size * a.dtype.itemsize for a in args) + sum(
        jnp.dtype(o[1]).itemsize * functools.reduce(lambda a, b: a * b, o[0]) for o in outs
    )
    shapes = [jax.ShapeDtypeStruct(s, d) for s, d in outs]
    return pl.pallas_call(
        kernel,
        out_shape=shapes,
        in_specs=[spaces.get(k, vm) for k in range(len(args))],
        out_specs=[(out_spaces or {}).get(k, vm) for k in range(len(outs))],
        scratch_shapes=list(scratch),
        compiler_params=pltpu.CompilerParams(vmem_limit_bytes=limit),
        cost_estimate=pl.CostEstimate(flops=flops, bytes_accessed=size, transcendentals=0),
    )(*args)


def pack_kernel(p, *refs):
    out_ref, block_ref, sems = refs[4], refs[9], refs[10]
    x_ref, dy_ref, route_ref, gate_ref = refs[5:9]
    fetches = [
        pltpu.make_async_copy(refs[k], refs[5 + k], sems.at[k]) for k in range(4)
    ]
    for fetch in fetches:
        fetch.start()
    for fetch in fetches:
        fetch.wait()
    in_y = lax.axis_index("yh") * p.nyl + lax.axis_index("yl")
    block = jnp.where(lax.axis_index("core") == 0, in_y, lax.axis_index("z"))
    top = p.full * LANES
    low = (iota((HALF, LANES), 1) == iota((HALF, LANES), 0)).astype(BF)
    high = (iota((HALF, LANES), 1) == iota((HALF, LANES), 0) + HALF).astype(BF)
    mixed = jnp.dot(x_ref[:, top:], low, preferred_element_type=F32) + jnp.dot(
        dy_ref[:, top:], high, preferred_element_type=F32
    )
    lanes = (iota((p.tok, LANES), 1) == iota((p.tok, LANES), 0) + block * p.tok).astype(BF)
    meta = jnp.concatenate(
        [route_ref[...].astype(F32), gate_ref[...].astype(F32)], axis=0
    ).astype(BF)
    placed = jnp.dot(meta, lanes, preferred_element_type=F32).astype(BF)
    t = p.tok
    for j in range(p.full):
        block_ref[j * t : (j + 1) * t, :] = x_ref[:, j * LANES : (j + 1) * LANES]
        k = p.full + 1 + j
        block_ref[k * t : (k + 1) * t, :] = dy_ref[:, j * LANES : (j + 1) * LANES]
    block_ref[p.full * t : (p.full + 1) * t, :] = mixed.astype(BF)
    block_ref[p.groups * t :, :] = placed
    stores = [
        pltpu.make_async_copy(block_ref, out_ref.at[b], sems.at[4 + b]) for b in range(p.nb)
    ]
    for store in stores:
        store.start()
    for store in stores:
        store.wait()


def slot_target(p, first):
    r = iota((p.grp, p.lanes), 0)
    b = iota((p.grp, p.lanes), 1) // p.tok
    c = r % p.c
    in_y = jnp.where((r // p.c == b % p.nyl) & (c // p.cap == b // p.nyl), c % p.cap, -2)
    in_z = jnp.where(r % p.nz == b, r // p.nz, -2)
    return jnp.where(first, in_y, in_z).astype(F32)


def one_hot(p, ranks, target, weight=1.0):
    eq = ranks[:, None, :] == target[None, :, :]
    return jnp.where(eq, weight, 0.0).astype(F32).reshape(-1, p.lanes).astype(BF)


def dispatch_kernel(p, in_ref, out_ref, rank_ref, held, sems):
    first = lax.axis_index("core") == 0
    yh, z = lax.axis_index("yh"), lax.axis_index("z")
    t = p.tok
    meta = in_ref[0, p.groups * t :, :].astype(F32)
    for b in range(1, p.nb):
        meta = meta + in_ref[b, p.groups * t :, :].astype(F32)
    q = iota((p.nq, p.lanes), 0)
    in_y = ((q // p.nz) * p.nyh + yh) * p.nz + q % p.nz
    in_z = (q // p.nyl) * p.nz + z
    expert = jnp.where(first, in_y, in_z).astype(F32)
    hit = jnp.zeros((p.nq, p.lanes), F32)
    gate = jnp.zeros((p.nq, p.lanes), F32)
    for k in range(p.picks):
        same = meta[k : k + 1, : p.lanes] == expert
        hit = hit + jnp.where(same, 1.0, 0.0)
        gate = gate + jnp.where(same, meta[p.picks + k : p.picks + k + 1, : p.lanes], 0.0)
    a, b = iota((p.lanes, p.lanes), 0), iota((p.lanes, p.lanes), 1)
    before = jnp.where((a < b) & (a // t == b // t), 1.0, 0.0).astype(BF)
    rank = jnp.dot(hit.astype(BF), before, preferred_element_type=F32)
    ranks = jnp.where(hit > 0.5, rank, -1.0)
    rank_ref[...] = ranks
    target = slot_target(p, first)
    pick = one_hot(p, ranks, target)
    gate = jnp.broadcast_to(gate[:, None, :], (p.nq, p.grp, p.lanes))
    scaled = one_hot(p, ranks, target, gate)
    left = iota((p.nq * p.grp, LANES), 1) < HALF
    stores = []
    for g in range(p.groups):
        feats = in_ref[:, g * t : (g + 1) * t, :].reshape(p.lanes, LANES)
        rows = jnp.dot(pick if g <= p.full else scaled, feats, preferred_element_type=F32)
        if g == p.full:
            both = jnp.dot(scaled, feats, preferred_element_type=F32)
            rows = jnp.where(left, rows, both)
        at = slice(g * p.grp, (g + 1) * p.grp)
        held[:, at, :] = rows.astype(BF).reshape(p.nq, p.grp, LANES)
        store = pltpu.make_async_copy(held.at[:, at, :], out_ref.at[:, at, :], sems.at[g])
        store.start()
        stores.append(store)
    for store in stores:
        store.wait()


def project_kernel(p, in_ref, wgu_ref, wd_hbm, x_ref, pre_ref, flat, dy, wd, sem):
    fetch = pltpu.make_async_copy(wd_hbm.at[: p.half_d], wd, sem)
    fetch.start()
    first = lax.axis_index("core") == 0

    def piece_in_y(group, yl):
        row = group * p.grp + yl * p.c
        return jnp.concatenate(
            [flat[pl.ds(row + c, p.nq, stride=p.pitch), :] for c in range(p.c)], axis=0
        )

    def blocks():
        for yh in range(p.nyh):
            for c in range(p.cap):
                for x in range(p.nx):
                    yield c, (x * p.nyh + yh) * p.nyl

    def piece_in_z(group, yl):
        rows = [(s + yl) * p.pitch + group * p.grp + c * p.nz for c, s in blocks()]
        return jnp.concatenate([flat[r : r + p.nz, :] for r in rows], axis=0)

    left = iota((p.rows, LANES), 1) < HALF

    def project(piece):
        for s in range(p.nq):
            flat[s * p.pitch : s * p.pitch + p.msg, :] = in_ref[s].astype(F32)
        for j in range(p.full):
            for yl in range(p.nyl):
                at = (j * p.nyl + yl) * LANES
                x_ref[:, at : at + LANES] = piece(j, yl).astype(BF)
                dy[:, at : at + LANES] = piece(p.full + 1 + j, yl).astype(BF)
        for u in range(p.ntail):
            at = (p.full * p.nyl + u) * LANES
            a = piece(p.full, 2 * u)
            b = piece(p.full, 2 * u + 1)
            x_ref[:, at : at + LANES] = jnp.where(left, a, pltpu.roll(b, HALF, 1)).astype(BF)
            dy[:, at : at + LANES] = jnp.where(left, pltpu.roll(a, HALF, 1), b).astype(BF)
        pre = jnp.dot(x_ref[...], wgu_ref[...], preferred_element_type=F32)
        fetch.wait()
        back = jnp.dot(dy[...], wd[...], preferred_element_type=F32)
        two, three = 2 * LANES, 3 * LANES
        pre_ref[:, :two] = pre[:, :two]
        pre_ref[:, two:three] = back[:, :LANES]
        pre_ref[:, three : three + two] = pre[:, two:]
        pre_ref[:, three + two :] = back[:, LANES:]

    @pl.when(first)
    def _():
        project(piece_in_y)

    @pl.when(jnp.logical_not(first))
    def _():
        project(piece_in_z)


def stash_kernel(in_ref, out_ref, sem):
    copy = pltpu.make_async_copy(in_ref, out_ref.at[: in_ref.shape[0]], sem)
    copy.start()
    copy.wait()


def back_kernel(p, pre_ref, got_ref, wgu_ref, out_ref, d_ref, flat, held, sems):
    two, three = 2 * LANES, 3 * LANES
    nt = (((1,), (1,)), ((), ()))
    tail = p.full * p.grp
    chunks = p.full * p.nyl
    parts = 4
    left = iota((p.nz, LANES), 1) < HALF
    for k in range(2):
        mine, theirs = k * three, (1 - k) * three

        def whole(at):
            own = pre_ref[:, mine + at : mine + at + LANES]
            return own + got_ref[:, theirs + at : theirs + at + LANES]

        pre_gate, pre_up, scaled = whole(0), whole(LANES), whole(two)
        sig = 1.0 / (1.0 + jnp.exp(-pre_gate))
        d_gate = scaled * pre_up * sig * (1.0 + pre_gate * (1.0 - sig))
        d_ref[:, k * two : k * two + LANES] = d_gate.astype(BF)
        d_ref[:, k * two + LANES : (k + 1) * two] = (scaled * pre_gate * sig).astype(BF)

    def part(k):
        at = k * LANES
        return lax.dot_general(
            d_ref[...], wgu_ref[at : at + LANES, :], nt, preferred_element_type=F32
        )

    def put_in_y(k, value):
        base = k * p.c if k < chunks else tail + (k - chunks) * p.c
        for c in range(p.c):
            flat[pl.ds(base + c, p.nq, stride=p.ret_pitch), :] = value[c * p.nq : (c + 1) * p.nq, :]

    def put_in_z(k, value):
        def block(yh, c, x):
            at = ((yh * p.cap + c) * p.nx + x) * p.nz
            return value[at : at + p.nz, :]

        for yh in range(p.nyh):
            for x in range(p.nx):
                s = (x * p.nyh + yh) * p.nyl
                if k < chunks:
                    for c in range(p.cap):
                        row = (s + k % p.nyl) * p.ret_pitch + k // p.nyl * p.grp + c * p.nz
                        flat[row : row + p.nz, :] = block(yh, c, x)
                    continue
                for c in range(0, p.cap, 2):
                    one = block(yh, c, x)
                    two = block(yh, c + 1, x) if c + 1 < p.cap else one
                    ends = (
                        jnp.where(left, one, pltpu.roll(two, HALF, 1)),
                        jnp.where(left, pltpu.roll(one, HALF, 1), two),
                    )
                    for h in range(2):
                        row = (s + 2 * (k - chunks) + h) * p.ret_pitch + tail + c // 2 * p.nz
                        flat[row : row + p.nz, :] = ends[h]

    def store():
        copies = []
        for k in range(parts):
            at = slice(k * p.nq // parts, (k + 1) * p.nq // parts)
            for s in range(at.start, at.stop):
                held[s] = flat[s * p.ret_pitch : s * p.ret_pitch + p.ret, :].astype(BF)
            copies.append(pltpu.make_async_copy(held.at[at], out_ref.at[at], sems.at[k]))
            copies[-1].start()
        for copy in copies:
            copy.wait()

    first = lax.axis_index("core") == 0

    @pl.when(first)
    def _():
        for r in range(tail + p.ntail * p.c, tail + p.tail):
            flat[pl.ds(r, p.nq, stride=p.ret_pitch), :] = jnp.zeros((p.nq, LANES), F32)
        for k in range(chunks + p.ntail):
            put_in_y(k, part(k))
        store()

    @pl.when(jnp.logical_not(first))
    def _():
        for k in range(chunks + p.ntail):
            put_in_z(k, part(k))
        store()


def combine_kernel(p, in_ref, pick_ref, ends_ref, out_ref):
    t = p.tok
    first = lax.axis_index("core") == 0
    for g in range(p.full):
        rows = in_ref[:, g * p.grp : (g + 1) * p.grp, :].reshape(p.nq * p.grp, LANES)
        total = jnp.dot(pick_ref[...], rows, preferred_element_type=F32)
        out_ref[:, g * t : (g + 1) * t, :] = total.astype(BF).reshape(p.nb, t, LANES)
    tail = p.full * p.grp

    def tail_total(lanes, start, rows):
        rows = in_ref[:, tail + start : tail + start + rows, :].reshape(-1, LANES)
        return jnp.dot(ends_ref[:, lanes], rows, preferred_element_type=F32)

    @pl.when(first)
    def _():
        last = tail_total(slice(0, p.nq * p.tail), 0, p.tail)
        for b in range(p.nb):
            src = (b // p.nyl) * p.nyl + (b % p.nyl) // 2
            out_ref[b, p.full * t :, :] = last[src * t : (src + 1) * t, :].astype(BF)

    @pl.when(jnp.logical_not(first))
    def _():
        sides = [None, None]
        n = p.nq * p.nz
        for c in range(p.cap):
            part = tail_total(slice(c * n, (c + 1) * n), c // 2 * p.nz, p.nz)
            sides[c % 2] = part if sides[c % 2] is None else sides[c % 2] + part
        last = sides[0] + pltpu.roll(sides[1], HALF, 1)
        out_ref[:, p.full * t :, :] = last.astype(BF).reshape(p.nb, t, LANES)


def finish_kernel(p, in_ref, out_ref):
    odd = jnp.where(lax.axis_index("core") == 0, lax.axis_index("yl") % 2, 0)
    total = in_ref[0].astype(F32)
    for b in range(1, p.nb):
        total = total + in_ref[b].astype(F32)
    t = p.tok
    for j in range(p.full):
        out_ref[:, j * LANES : (j + 1) * LANES] = total[j * t : (j + 1) * t, :].astype(BF)
    tail = total[p.full * t :, :]
    tail = jnp.where(odd == 1, pltpu.roll(tail, HALF, 1), tail)
    out_ref[:, p.full * LANES :] = tail[:, :HALF].astype(BF)


def grads_kernel(p, x_ref, d_ref, rank_ref, mine_ref, other_ref, pick_ref, ends_ref):
    first = lax.axis_index("core") == 0
    eq = rank_ref[...][:, None, :] == slot_target(p, first)[None, :, :]
    pick = jnp.where(eq, 1.0, 0.0).astype(F32)

    def turned(rows):
        return rows.reshape(-1, p.lanes).T.astype(BF)

    pick_ref[...] = turned(pick)

    @pl.when(first)
    def _():
        ends_ref[:, : p.nq * p.tail] = turned(pick[:, : p.tail, :])

    @pl.when(jnp.logical_not(first))
    def _():
        n = p.nq * p.nz
        for c in range(p.cap):
            ends_ref[:, c * n : (c + 1) * n] = turned(pick[:, c * p.nz : (c + 1) * p.nz, :])

    tn = (((0,), (0,)), ((), ()))

    def put(yl, at, size, src, got, k):
        mine_ref[k, yl, at : at + size, :] = got[src : src + size, k * LANES : (k + 1) * LANES]

    def put_other(yl, at, size, src, got):
        other_ref[yl, at : at + size, :] = got[src : src + size, :]

    for k in range(p.full * p.nyl + p.ntail):
        x = x_ref[:, k * LANES : (k + 1) * LANES]
        both = lax.dot_general(x, d_ref[...], tn, preferred_element_type=F32).astype(BF)
        mine, other = both[:, : 2 * LANES], both[:, 2 * LANES :]
        if k < p.full * p.nyl:
            spots = [(k % p.nyl, (k // p.nyl) * LANES, LANES, 0)]
        else:
            u = k - p.full * p.nyl
            spots = [(2 * u + h, p.full * LANES, HALF, h * HALF) for h in range(2)]
        for spot in spots:
            put(*spot, mine, 0)
            put(*spot, mine, 1)
            put_other(*spot, other)


def assemble_kernel(p, mine_ref, got_ref, gate_ref, up_ref):
    core = lax.axis_index("core")
    for yl in range(p.nyl):
        gate_ref[yl, core] = mine_ref[0, yl]
        up_ref[yl, core] = mine_ref[1, yl]
        gate_ref[yl, 1 - core] = got_ref[yl, :, :LANES]
        up_ref[yl, 1 - core] = got_ref[yl, :, LANES:]


def lane_tiles(p, w):
    top = p.full * LANES
    n = w.shape[-1]
    tiles = w[:, :top].reshape(p.nyl, p.full, LANES, n).transpose(1, 0, 2, 3).reshape(-1, n)
    return jnp.concatenate([tiles, w[:, top:].reshape(-1, n)], axis=0)


def body(sizes, *args):
    return program(sizes, *args)


def program(sizes, tokens, grad_out, gate_weights, routing, w_gate, w_up, w_down):
    p = Plan(sizes, *routing.shape, tokens.shape[1])
    swap = [(0, 1), (1, 0)]
    core = lax.axis_index("core")
    bind = functools.partial

    def exchange(v):
        return lax.ppermute(v, "core", swap)

    def all_to_all(v, groups):
        return lax.all_to_all(
            v, AXES, split_axis=0, concat_axis=0, axis_index_groups=groups, tiled=True
        )

    column_groups, plane_groups = p.column_groups(), p.plane_groups()

    (pre,) = call(
        bind(pack_kernel, p),
        [((p.nb, p.pre, LANES), BF)],
        (tokens, grad_out, routing.T, gate_weights.T),
        scratch=[
            pltpu.VMEM(tokens.shape, BF),
            pltpu.VMEM(grad_out.shape, BF),
            pltpu.VMEM(routing.shape[::-1], routing.dtype),
            pltpu.VMEM(gate_weights.shape[::-1], BF),
            pltpu.VMEM((p.pre, LANES), BF),
            pltpu.SemaphoreType.DMA((4 + p.nb,)),
        ],
        out_spaces={0: HBM},
        spaces={k: HBM for k in range(4)},
        limit=VMEM_ALL,
    )
    column = all_to_all(pre, column_groups)

    w_gate, w_up, w_down = lax.optimization_barrier((w_gate, w_up, w_down, pre))[:3]
    shape = (p.nyl, p.nc, p.part_w, LANES)
    weights = jnp.stack(
        [w_gate[0].reshape(shape), w_up[0].reshape(shape), w_down[0].T.reshape(shape)]
    )
    mine = lax.dynamic_index_in_dim(weights, core, axis=2, keepdims=False)
    other = lax.dynamic_index_in_dim(weights, 1 - core, axis=2, keepdims=False)
    theirs = exchange(other)
    wgu = lane_tiles(p, jnp.concatenate([mine[0], mine[1], theirs[0], theirs[1]], axis=-1))
    wd = lane_tiles(p, jnp.concatenate([mine[2], theirs[2]], axis=-1))
    (wd,) = call(
        stash_kernel,
        [((STASH_ROWS, 2 * LANES), BF)],
        (wd,),
        scratch=[pltpu.SemaphoreType.DMA],
        out_spaces={0: HBM},
        limit=3 * VMEM_LIMIT,
    )

    sent, ranks = call(
        bind(dispatch_kernel, p),
        [((p.nq, p.msg, LANES), BF), ((p.nq, p.lanes), F32)],
        (column,),
        scratch=[
            pltpu.VMEM((p.nq, p.msg, LANES), BF),
            pltpu.SemaphoreType.DMA((p.groups,)),
        ],
        out_spaces={0: HBM},
    )
    received = all_to_all(sent, plane_groups)
    rows_x, partial = call(
        bind(project_kernel, p),
        [
            ((p.rows, p.half_d), BF),
            ((p.rows, 6 * LANES), F32),
        ],
        (received, wgu, wd),
        scratch=[
            pltpu.VMEM(((p.nq + 1) * p.pitch, LANES), F32),
            pltpu.VMEM((p.rows, p.half_d), BF),
            pltpu.VMEM((p.half_d, 2 * LANES), BF),
            pltpu.SemaphoreType.DMA,
        ],
        spaces={2: HBM},
        limit=3 * VMEM_LIMIT,
    )
    back, d_all = call(
        bind(back_kernel, p),
        [((p.nq, p.ret, LANES), BF), ((p.rows, 4 * LANES), BF)],
        (partial, exchange(partial), wgu),
        scratch=[
            pltpu.VMEM(((p.nq + 1) * p.ret_pitch, LANES), F32),
            pltpu.VMEM((p.nq, p.ret, LANES), BF),
            pltpu.SemaphoreType.DMA((4,)),
        ],
        out_spaces={0: HBM},
    )
    returned = all_to_all(back, plane_groups)
    rows_x, d_all = lax.optimization_barrier((rows_x, d_all, back))[:2]
    chosen = ((p.lanes, p.nq * p.grp), BF)
    grad_mine, grad_other, pick, ends = call(
        bind(grads_kernel, p),
        [((2, p.nyl, p.part_w, LANES), BF), ((p.nyl, p.part_w, 2 * LANES), BF), chosen, chosen],
        (rows_x, d_all, ranks),
    )
    grad_got = exchange(grad_other)
    (share,) = call(bind(combine_kernel, p), [((p.nb, p.fin, LANES), BF)], (returned, pick, ends))
    last = all_to_all(share, column_groups)
    grad_mine, grad_got = lax.optimization_barrier((grad_mine, grad_got, share))[:2]
    grad_g, grad_u = call(
        bind(assemble_kernel, p), [(shape, BF), (shape, BF)], (grad_mine, grad_got)
    )
    (grad_tokens,) = call(bind(finish_kernel, p), [((p.tok, p.part_w), BF)], (last,))
    out = (1, p.nyl * p.nc * p.part_w, LANES)
    return grad_tokens, grad_g.reshape(out), grad_u.reshape(out)


def solution(mesh):
    sizes = axis_sizes(mesh.shape["expert"], mesh.shape["tensor"])
    inner = Mesh(mesh.devices.reshape(sizes), AXES)
    ex, te = AXES[:3], AXES[3:]
    placed = (
        P(ex, te),
        P(ex, te),
        P(ex, None),
        P(ex, None),
        P(ex, None, te),
        P(ex, None, te),
        P(ex, te, None),
    )
    return jax.shard_map(
        functools.partial(body, sizes),
        mesh=inner,
        in_specs=placed,
        out_specs=(P(ex, te), P(ex, None, te), P(ex, None, te)),
        check_vma=False,
    )
```

```python
import functools

import jax
import jax.numpy as jnp
from jax import lax
from jax.experimental import pallas as pl
from jax.experimental.pallas import tpu as pltpu
from jax.sharding import Mesh, PartitionSpec as P

BF = jnp.bfloat16
F32 = jnp.float32
AXES = ("x", "yh", "z", "yl", "core")
LANES = 128
HALF = 64
VMEM_LIMIT = 16 * 1024 * 1024
STASH_ROWS = 40 * 1024
VMEM_ALL = 67043328
HBM = pl.BlockSpec(memory_space=pltpu.MemorySpace.HBM)


def axis_sizes(experts, tensor):
    if (experts, tensor) == (64, 8):
        return (4, 2, 8, 4, 2)
    assert experts % 2 == 0 and tensor == experts
    return (2, 1, experts // 2, tensor // 2, 2)


def pitch(rows):
    tiles = -(-rows // 8)
    return 8 * (tiles + 1 - tiles % 2)


class Plan:
    def __init__(self, sizes, tok_rows, picks, part_w):
        self.nx, self.nyh, self.nz, self.nyl, self.nc = sizes
        self.tok, self.picks, self.part_w = tok_rows, picks, part_w
        experts = self.nx * self.nyh * self.nz
        self.cap = 3 * tok_rows * picks // (2 * experts)
        self.nb = self.nyh * self.nyl
        assert self.nb == self.nz
        self.nq = self.nx * self.nb
        self.full = part_w // LANES
        assert part_w == self.full * LANES + HALF
        self.groups = 2 * self.full + 1
        self.lanes = self.nb * tok_rows
        self.c = self.nyh * self.cap
        self.grp = self.nb * self.cap
        self.rows = self.nq * self.c
        self.msg = self.groups * self.grp
        self.pitch = pitch(self.msg)
        self.ntail = self.nyl // 2
        self.pairs = (self.cap + 1) // 2
        self.tail = -(-max(self.ntail * self.c, self.pairs * self.nz) // 8) * 8
        self.ret = self.full * self.grp + self.tail
        self.ret_pitch = pitch(self.ret)
        self.half_d = self.nyl * part_w
        self.pre = self.groups * tok_rows + 2 * picks
        self.fin = (self.full + 1) * tok_rows

    def device(self, x, yh, z, yl, core):
        return (((x * self.nyh + yh) * self.nz + z) * self.nyl + yl) * self.nc + core

    def column_groups(self):
        xs, yhs, zs, yls = map(range, (self.nx, self.nyh, self.nz, self.nyl))
        first = [[self.device(x, h, z, l, 0) for h in yhs for l in yls] for x in xs for z in zs]
        second = [
            [self.device(x, h, z, l, 1) for z in zs] for x in xs for h in yhs for l in yls
        ]
        return first + second

    def plane_groups(self):
        xs, yhs, zs, yls = map(range, (self.nx, self.nyh, self.nz, self.nyl))
        first = [[self.device(x, h, z, l, 0) for x in xs for z in zs] for h in yhs for l in yls]
        second = [[self.device(x, h, z, l, 1) for x in xs for h in yhs for l in yls] for z in zs]
        return first + second


def iota(shape, dim):
    return lax.broadcasted_iota(jnp.int32, shape, dim)


def call(kernel, outs, args, scratch=(), flops=0, spaces=None, limit=VMEM_LIMIT, out_spaces=None):
    vm = pl.BlockSpec(memory_space=pltpu.VMEM)
    spaces = spaces or {}
    size = sum(a.size * a.dtype.itemsize for a in args) + sum(
        jnp.dtype(o[1]).itemsize * functools.reduce(lambda a, b: a * b, o[0]) for o in outs
    )
    shapes = [jax.ShapeDtypeStruct(s, d) for s, d in outs]
    return pl.pallas_call(
        kernel,
        out_shape=shapes,
        in_specs=[spaces.get(k, vm) for k in range(len(args))],
        out_specs=[(out_spaces or {}).get(k, vm) for k in range(len(outs))],
        scratch_shapes=list(scratch),
        compiler_params=pltpu.CompilerParams(vmem_limit_bytes=limit),
        cost_estimate=pl.CostEstimate(flops=flops, bytes_accessed=size, transcendentals=0),
    )(*args)


def pack_kernel(p, *refs):
    out_ref, block_ref, sems = refs[4], refs[9], refs[10]
    x_ref, dy_ref, route_ref, gate_ref = refs[5:9]
    fetches = [
        pltpu.make_async_copy(refs[k], refs[5 + k], sems.at[k]) for k in range(4)
    ]
    for fetch in fetches:
        fetch.start()
    for fetch in fetches:
        fetch.wait()
    in_y = lax.axis_index("yh") * p.nyl + lax.axis_index("yl")
    block = jnp.where(lax.axis_index("core") == 0, in_y, lax.axis_index("z"))
    top = p.full * LANES
    low = (iota((HALF, LANES), 1) == iota((HALF, LANES), 0)).astype(BF)
    high = (iota((HALF, LANES), 1) == iota((HALF, LANES), 0) + HALF).astype(BF)
    mixed = jnp.dot(x_ref[:, top:], low, preferred_element_type=F32) + jnp.dot(
        dy_ref[:, top:], high, preferred_element_type=F32
    )
    lanes = (iota((p.tok, LANES), 1) == iota((p.tok, LANES), 0) + block * p.tok).astype(BF)
    meta = jnp.concatenate(
        [route_ref[...].astype(F32), gate_ref[...].astype(F32)], axis=0
    ).astype(BF)
    placed = jnp.dot(meta, lanes, preferred_element_type=F32).astype(BF)
    t = p.tok
    for j in range(p.full):
        block_ref[j * t : (j + 1) * t, :] = x_ref[:, j * LANES : (j + 1) * LANES]
        k = p.full + 1 + j
        block_ref[k * t : (k + 1) * t, :] = dy_ref[:, j * LANES : (j + 1) * LANES]
    block_ref[p.full * t : (p.full + 1) * t, :] = mixed.astype(BF)
    block_ref[p.groups * t :, :] = placed
    stores = [
        pltpu.make_async_copy(block_ref, out_ref.at[b], sems.at[4 + b]) for b in range(p.nb)
    ]
    for store in stores:
        store.start()
    for store in stores:
        store.wait()


def slot_target(p, first):
    r = iota((p.grp, p.lanes), 0)
    b = iota((p.grp, p.lanes), 1) // p.tok
    c = r % p.c
    in_y = jnp.where((r // p.c == b % p.nyl) & (c // p.cap == b // p.nyl), c % p.cap, -2)
    in_z = jnp.where(r % p.nz == b, r // p.nz, -2)
    return jnp.where(first, in_y, in_z).astype(F32)


def one_hot(p, ranks, target, weight=1.0):
    eq = ranks[:, None, :] == target[None, :, :]
    return jnp.where(eq, weight, 0.0).astype(F32).reshape(-1, p.lanes).astype(BF)


def dispatch_kernel(p, in_ref, out_ref, rank_ref, held, sems):
    first = lax.axis_index("core") == 0
    yh, z = lax.axis_index("yh"), lax.axis_index("z")
    t = p.tok
    meta = in_ref[0, p.groups * t :, :].astype(F32)
    for b in range(1, p.nb):
        meta = meta + in_ref[b, p.groups * t :, :].astype(F32)
    q = iota((p.nq, p.lanes), 0)
    in_y = ((q // p.nz) * p.nyh + yh) * p.nz + q % p.nz
    in_z = (q // p.nyl) * p.nz + z
    expert = jnp.where(first, in_y, in_z).astype(F32)
    hit = jnp.zeros((p.nq, p.lanes), F32)
    gate = jnp.zeros((p.nq, p.lanes), F32)
    for k in range(p.picks):
        same = meta[k : k + 1, : p.lanes] == expert
        hit = hit + jnp.where(same, 1.0, 0.0)
        gate = gate + jnp.where(same, meta[p.picks + k : p.picks + k + 1, : p.lanes], 0.0)
    a, b = iota((p.lanes, p.lanes), 0), iota((p.lanes, p.lanes), 1)
    before = jnp.where((a < b) & (a // t == b // t), 1.0, 0.0).astype(BF)
    rank = jnp.dot(hit.astype(BF), before, preferred_element_type=F32)
    ranks = jnp.where(hit > 0.5, rank, -1.0)
    rank_ref[...] = ranks
    target = slot_target(p, first)
    pick = one_hot(p, ranks, target)
    gate = jnp.broadcast_to(gate[:, None, :], (p.nq, p.grp, p.lanes))
    scaled = one_hot(p, ranks, target, gate)
    left = iota((p.nq * p.grp, LANES), 1) < HALF
    stores = []
    for g in range(p.groups):
        feats = in_ref[:, g * t : (g + 1) * t, :].reshape(p.lanes, LANES)
        rows = jnp.dot(pick if g <= p.full else scaled, feats, preferred_element_type=F32)
        if g == p.full:
            both = jnp.dot(scaled, feats, preferred_element_type=F32)
            rows = jnp.where(left, rows, both)
        at = slice(g * p.grp, (g + 1) * p.grp)
        held[:, at, :] = rows.astype(BF).reshape(p.nq, p.grp, LANES)
        store = pltpu.make_async_copy(held.at[:, at, :], out_ref.at[:, at, :], sems.at[g])
        store.start()
        stores.append(store)
    for store in stores:
        store.wait()


def project_kernel(p, in_ref, wgu_ref, wd_hbm, x_ref, pre_ref, send_ref, flat, dy, wd, sem):
    fetch = pltpu.make_async_copy(wd_hbm.at[: p.half_d], wd, sem)
    fetch.start()
    first = lax.axis_index("core") == 0

    def piece_in_y(group, yl):
        row = group * p.grp + yl * p.c
        return jnp.concatenate(
            [flat[pl.ds(row + c, p.nq, stride=p.pitch), :] for c in range(p.c)], axis=0
        )

    def blocks():
        for yh in range(p.nyh):
            for c in range(p.cap):
                for x in range(p.nx):
                    yield c, (x * p.nyh + yh) * p.nyl

    def piece_in_z(group, yl):
        rows = [(s + yl) * p.pitch + group * p.grp + c * p.nz for c, s in blocks()]
        return jnp.concatenate([flat[r : r + p.nz, :] for r in rows], axis=0)

    left = iota((p.rows, LANES), 1) < HALF

    def project(piece):
        for s in range(p.nq):
            flat[s * p.pitch : s * p.pitch + p.msg, :] = in_ref[s].astype(F32)
        for j in range(p.full):
            for yl in range(p.nyl):
                at = (j * p.nyl + yl) * LANES
                x_ref[:, at : at + LANES] = piece(j, yl).astype(BF)
                dy[:, at : at + LANES] = piece(p.full + 1 + j, yl).astype(BF)
        for u in range(p.ntail):
            at = (p.full * p.nyl + u) * LANES
            a = piece(p.full, 2 * u)
            b = piece(p.full, 2 * u + 1)
            x_ref[:, at : at + LANES] = jnp.where(left, a, pltpu.roll(b, HALF, 1)).astype(BF)
            dy[:, at : at + LANES] = jnp.where(left, pltpu.roll(a, HALF, 1), b).astype(BF)
        pre = jnp.dot(x_ref[...], wgu_ref[...], preferred_element_type=F32)
        fetch.wait()
        back = jnp.dot(dy[...], wd[...], preferred_element_type=F32)
        two, three = 2 * LANES, 3 * LANES
        pre_ref[:, :two] = pre[:, :two]
        pre_ref[:, two:three] = back[:, :LANES]
        pre_ref[:, three : three + two] = pre[:, two:]
        pre_ref[:, three + two :] = back[:, LANES:]
        send_ref[...] = pre_ref[...].astype(BF)

    @pl.when(first)
    def _():
        project(piece_in_y)

    @pl.when(jnp.logical_not(first))
    def _():
        project(piece_in_z)


def stash_kernel(in_ref, out_ref, sem):
    copy = pltpu.make_async_copy(in_ref, out_ref.at[: in_ref.shape[0]], sem)
    copy.start()
    copy.wait()


def back_kernel(p, pre_ref, got_ref, wgu_ref, out_ref, d_ref, flat, held, sems):
    two, three = 2 * LANES, 3 * LANES
    nt = (((1,), (1,)), ((), ()))
    tail = p.full * p.grp
    chunks = p.full * p.nyl
    left = iota((p.nz, LANES), 1) < HALF
    for k in range(2):
        mine, theirs = k * three, (1 - k) * three

        def whole(at):
            own = pre_ref[:, mine + at : mine + at + LANES]
            return own + got_ref[:, theirs + at : theirs + at + LANES].astype(F32)

        pre_gate, pre_up, scaled = whole(0), whole(LANES), whole(two)
        sig = 1.0 / (1.0 + jnp.exp(-pre_gate))
        d_gate = scaled * pre_up * sig * (1.0 + pre_gate * (1.0 - sig))
        d_ref[:, k * two : k * two + LANES] = d_gate.astype(BF)
        d_ref[:, k * two + LANES : (k + 1) * two] = (scaled * pre_gate * sig).astype(BF)

    def part(k):
        at = k * LANES
        return lax.dot_general(
            d_ref[...], wgu_ref[at : at + LANES, :], nt, preferred_element_type=F32
        )

    def put_in_y(k, value):
        base = k * p.c if k < chunks else tail + (k - chunks) * p.c
        for c in range(p.c):
            flat[pl.ds(base + c, p.nq, stride=p.ret_pitch), :] = value[c * p.nq : (c + 1) * p.nq, :]

    def put_in_z(k, value):
        def block(yh, c, x):
            at = ((yh * p.cap + c) * p.nx + x) * p.nz
            return value[at : at + p.nz, :]

        for yh in range(p.nyh):
            for x in range(p.nx):
                s = (x * p.nyh + yh) * p.nyl
                if k < chunks:
                    for c in range(p.cap):
                        row = (s + k % p.nyl) * p.ret_pitch + k // p.nyl * p.grp + c * p.nz
                        flat[row : row + p.nz, :] = block(yh, c, x)
                    continue
                for c in range(0, p.cap, 2):
                    one = block(yh, c, x)
                    two = block(yh, c + 1, x) if c + 1 < p.cap else one
                    ends = (
                        jnp.where(left, one, pltpu.roll(two, HALF, 1)),
                        jnp.where(left, pltpu.roll(one, HALF, 1), two),
                    )
                    for h in range(2):
                        row = (s + 2 * (k - chunks) + h) * p.ret_pitch + tail + c // 2 * p.nz
                        flat[row : row + p.nz, :] = ends[h]

    def rows_of(g):
        return slice(g * p.grp, (g + 1) * p.grp if g < p.full else p.ret)

    def store(g):
        at = rows_of(g)
        for s in range(p.nq):
            base = s * p.ret_pitch
            held[s, at, :] = flat[base + at.start : base + at.stop, :].astype(BF)
        copy = pltpu.make_async_copy(held.at[:, at, :], out_ref.at[:, at, :], sems.at[g])
        copy.start()
        return copy

    def run(put):
        copies = []
        for g in range(p.full):
            for yl in range(p.nyl):
                put(g * p.nyl + yl, part(g * p.nyl + yl))
            copies.append(store(g))
        for u in range(p.ntail):
            put(chunks + u, part(chunks + u))
        copies.append(store(p.full))
        for copy in copies:
            copy.wait()

    first = lax.axis_index("core") == 0

    @pl.when(first)
    def _():
        for r in range(tail + p.ntail * p.c, tail + p.tail):
            flat[pl.ds(r, p.nq, stride=p.ret_pitch), :] = jnp.zeros((p.nq, LANES), F32)
        run(put_in_y)

    @pl.when(jnp.logical_not(first))
    def _():
        run(put_in_z)


def combine_kernel(p, in_ref, pick_ref, ends_ref, out_ref):
    t = p.tok
    first = lax.axis_index("core") == 0
    for g in range(p.full):
        rows = in_ref[:, g * p.grp : (g + 1) * p.grp, :].reshape(p.nq * p.grp, LANES)
        total = jnp.dot(pick_ref[...], rows, preferred_element_type=F32)
        out_ref[:, g * t : (g + 1) * t, :] = total.astype(BF).reshape(p.nb, t, LANES)
    tail = p.full * p.grp

    def tail_total(lanes, start, rows):
        rows = in_ref[:, tail + start : tail + start + rows, :].reshape(-1, LANES)
        return jnp.dot(ends_ref[:, lanes], rows, preferred_element_type=F32)

    @pl.when(first)
    def _():
        last = tail_total(slice(0, p.nq * p.tail), 0, p.tail)
        for b in range(p.nb):
            src = (b // p.nyl) * p.nyl + (b % p.nyl) // 2
            out_ref[b, p.full * t :, :] = last[src * t : (src + 1) * t, :].astype(BF)

    @pl.when(jnp.logical_not(first))
    def _():
        sides = [None, None]
        n = p.nq * p.nz
        for c in range(p.cap):
            part = tail_total(slice(c * n, (c + 1) * n), c // 2 * p.nz, p.nz)
            sides[c % 2] = part if sides[c % 2] is None else sides[c % 2] + part
        last = sides[0] + pltpu.roll(sides[1], HALF, 1)
        out_ref[:, p.full * t :, :] = last.astype(BF).reshape(p.nb, t, LANES)


def finish_kernel(p, in_ref, out_ref):
    odd = jnp.where(lax.axis_index("core") == 0, lax.axis_index("yl") % 2, 0)
    total = in_ref[0].astype(F32)
    for b in range(1, p.nb):
        total = total + in_ref[b].astype(F32)
    t = p.tok
    for j in range(p.full):
        out_ref[:, j * LANES : (j + 1) * LANES] = total[j * t : (j + 1) * t, :].astype(BF)
    tail = total[p.full * t :, :]
    tail = jnp.where(odd == 1, pltpu.roll(tail, HALF, 1), tail)
    out_ref[:, p.full * LANES :] = tail[:, :HALF].astype(BF)


def grads_kernel(p, x_ref, d_ref, rank_ref, mine_ref, other_ref, pick_ref, ends_ref):
    first = lax.axis_index("core") == 0
    eq = rank_ref[...][:, None, :] == slot_target(p, first)[None, :, :]
    pick = jnp.where(eq, 1.0, 0.0).astype(F32)

    def turned(rows):
        return rows.reshape(-1, p.lanes).T.astype(BF)

    pick_ref[...] = turned(pick)

    @pl.when(first)
    def _():
        ends_ref[:, : p.nq * p.tail] = turned(pick[:, : p.tail, :])

    @pl.when(jnp.logical_not(first))
    def _():
        n = p.nq * p.nz
        for c in range(p.cap):
            ends_ref[:, c * n : (c + 1) * n] = turned(pick[:, c * p.nz : (c + 1) * p.nz, :])

    tn = (((0,), (0,)), ((), ()))

    def put(yl, at, size, src, got, k):
        mine_ref[k, yl, at : at + size, :] = got[src : src + size, k * LANES : (k + 1) * LANES]

    def put_other(yl, at, size, src, got):
        other_ref[yl, at : at + size, :] = got[src : src + size, :]

    for k in range(p.full * p.nyl + p.ntail):
        x = x_ref[:, k * LANES : (k + 1) * LANES]
        both = lax.dot_general(x, d_ref[...], tn, preferred_element_type=F32).astype(BF)
        mine, other = both[:, : 2 * LANES], both[:, 2 * LANES :]
        if k < p.full * p.nyl:
            spots = [(k % p.nyl, (k // p.nyl) * LANES, LANES, 0)]
        else:
            u = k - p.full * p.nyl
            spots = [(2 * u + h, p.full * LANES, HALF, h * HALF) for h in range(2)]
        for spot in spots:
            put(*spot, mine, 0)
            put(*spot, mine, 1)
            put_other(*spot, other)


def assemble_kernel(p, mine_ref, got_ref, gate_ref, up_ref):
    core = lax.axis_index("core")
    for yl in range(p.nyl):
        gate_ref[yl, core] = mine_ref[0, yl]
        up_ref[yl, core] = mine_ref[1, yl]
        gate_ref[yl, 1 - core] = got_ref[yl, :, :LANES]
        up_ref[yl, 1 - core] = got_ref[yl, :, LANES:]


def lane_tiles(p, w):
    top = p.full * LANES
    n = w.shape[-1]
    tiles = w[:, :top].reshape(p.nyl, p.full, LANES, n).transpose(1, 0, 2, 3).reshape(-1, n)
    return jnp.concatenate([tiles, w[:, top:].reshape(-1, n)], axis=0)


def body(sizes, *args):
    return program(sizes, *args)


def program(sizes, tokens, grad_out, gate_weights, routing, w_gate, w_up, w_down):
    p = Plan(sizes, *routing.shape, tokens.shape[1])
    swap = [(0, 1), (1, 0)]
    core = lax.axis_index("core")
    bind = functools.partial

    def exchange(v):
        return lax.ppermute(v, "core", swap)

    def all_to_all(v, groups):
        return lax.all_to_all(
            v, AXES, split_axis=0, concat_axis=0, axis_index_groups=groups, tiled=True
        )

    column_groups, plane_groups = p.column_groups(), p.plane_groups()

    (pre,) = call(
        bind(pack_kernel, p),
        [((p.nb, p.pre, LANES), BF)],
        (tokens, grad_out, routing.T, gate_weights.T),
        scratch=[
            pltpu.VMEM(tokens.shape, BF),
            pltpu.VMEM(grad_out.shape, BF),
            pltpu.VMEM(routing.shape[::-1], routing.dtype),
            pltpu.VMEM(gate_weights.shape[::-1], BF),
            pltpu.VMEM((p.pre, LANES), BF),
            pltpu.SemaphoreType.DMA((4 + p.nb,)),
        ],
        out_spaces={0: HBM},
        spaces={k: HBM for k in range(4)},
        limit=VMEM_ALL,
    )
    column = all_to_all(pre, column_groups)

    w_gate, w_up, w_down = lax.optimization_barrier((w_gate, w_up, w_down, pre))[:3]
    shape = (p.nyl, p.nc, p.part_w, LANES)
    weights = jnp.stack(
        [w_gate[0].reshape(shape), w_up[0].reshape(shape), w_down[0].T.reshape(shape)]
    )
    mine = lax.dynamic_index_in_dim(weights, core, axis=2, keepdims=False)
    other = lax.dynamic_index_in_dim(weights, 1 - core, axis=2, keepdims=False)
    theirs = exchange(other)
    wgu = lane_tiles(p, jnp.concatenate([mine[0], mine[1], theirs[0], theirs[1]], axis=-1))
    wd = lane_tiles(p, jnp.concatenate([mine[2], theirs[2]], axis=-1))
    (wd,) = call(
        stash_kernel,
        [((STASH_ROWS, 2 * LANES), BF)],
        (wd,),
        scratch=[pltpu.SemaphoreType.DMA],
        out_spaces={0: HBM},
        limit=3 * VMEM_LIMIT,
    )

    sent, ranks = call(
        bind(dispatch_kernel, p),
        [((p.nq, p.msg, LANES), BF), ((p.nq, p.lanes), F32)],
        (column,),
        scratch=[
            pltpu.VMEM((p.nq, p.msg, LANES), BF),
            pltpu.SemaphoreType.DMA((p.groups,)),
        ],
        out_spaces={0: HBM},
    )
    received = all_to_all(sent, plane_groups)
    rows_x, partial, crossing = call(
        bind(project_kernel, p),
        [
            ((p.rows, p.half_d), BF),
            ((p.rows, 6 * LANES), F32),
            ((p.rows, 6 * LANES), BF),
        ],
        (received, wgu, wd),
        scratch=[
            pltpu.VMEM(((p.nq + 1) * p.pitch, LANES), F32),
            pltpu.VMEM((p.rows, p.half_d), BF),
            pltpu.VMEM((p.half_d, 2 * LANES), BF),
            pltpu.SemaphoreType.DMA,
        ],
        spaces={2: HBM},
        limit=3 * VMEM_LIMIT,
    )
    back, d_all = call(
        bind(back_kernel, p),
        [((p.nq, p.ret, LANES), BF), ((p.rows, 4 * LANES), BF)],
        (partial, exchange(crossing), wgu),
        scratch=[
            pltpu.VMEM(((p.nq + 1) * p.ret_pitch, LANES), F32),
            pltpu.VMEM((p.nq, p.ret, LANES), BF),
            pltpu.SemaphoreType.DMA((p.full + 1,)),
        ],
        out_spaces={0: HBM},
    )
    returned = all_to_all(back, plane_groups)
    rows_x, d_all = lax.optimization_barrier((rows_x, d_all, back))[:2]
    chosen = ((p.lanes, p.nq * p.grp), BF)
    grad_mine, grad_other, pick, ends = call(
        bind(grads_kernel, p),
        [((2, p.nyl, p.part_w, LANES), BF), ((p.nyl, p.part_w, 2 * LANES), BF), chosen, chosen],
        (rows_x, d_all, ranks),
    )
    grad_got = exchange(grad_other)
    (share,) = call(bind(combine_kernel, p), [((p.nb, p.fin, LANES), BF)], (returned, pick, ends))
    last = all_to_all(share, column_groups)
    grad_mine, grad_got = lax.optimization_barrier((grad_mine, grad_got, share))[:2]
    grad_g, grad_u = call(
        bind(assemble_kernel, p), [(shape, BF), (shape, BF)], (grad_mine, grad_got)
    )
    (grad_tokens,) = call(bind(finish_kernel, p), [((p.tok, p.part_w), BF)], (last,))
    out = (1, p.nyl * p.nc * p.part_w, LANES)
    return grad_tokens, grad_g.reshape(out), grad_u.reshape(out)


def solution(mesh):
    sizes = axis_sizes(mesh.shape["expert"], mesh.shape["tensor"])
    inner = Mesh(mesh.devices.reshape(sizes), AXES)
    ex, te = AXES[:3], AXES[3:]
    placed = (
        P(ex, te),
        P(ex, te),
        P(ex, None),
        P(ex, None),
        P(ex, None, te),
        P(ex, None, te),
        P(ex, te, None),
    )
    return jax.shard_map(
        functools.partial(body, sizes),
        mesh=inner,
        in_specs=placed,
        out_specs=(P(ex, te), P(ex, None, te), P(ex, None, te)),
        check_vma=False,
    )
```

```python
import functools

import jax
import jax.numpy as jnp
from jax import lax
from jax.experimental import pallas as pl
from jax.experimental.pallas import tpu as pltpu
from jax.sharding import Mesh, PartitionSpec as P

BF = jnp.bfloat16
F32 = jnp.float32
AXES = ("x", "yh", "z", "yl", "core")
LANES = 128
HALF = 64
Y_CORE = 1
VMEM_LIMIT = 16 * 1024 * 1024
STASH_ROWS = 40 * 1024
VMEM_ALL = 67043328
HBM = pl.BlockSpec(memory_space=pltpu.MemorySpace.HBM)


def axis_sizes(experts, tensor):
    if (experts, tensor) == (64, 8):
        return (4, 2, 8, 4, 2)
    assert experts % 2 == 0 and tensor == experts
    return (2, 1, experts // 2, tensor // 2, 2)


def pitch(rows):
    tiles = -(-rows // 8)
    return 8 * (tiles + 1 - tiles % 2)


class Plan:
    def __init__(self, sizes, tok_rows, picks, part_w):
        self.nx, self.nyh, self.nz, self.nyl, self.nc = sizes
        self.tok, self.picks, self.part_w = tok_rows, picks, part_w
        experts = self.nx * self.nyh * self.nz
        self.cap = 3 * tok_rows * picks // (2 * experts)
        self.nb = self.nyh * self.nyl
        assert self.nb == self.nz
        self.nq = self.nx * self.nb
        self.full = part_w // LANES
        assert part_w == self.full * LANES + HALF
        self.groups = 2 * self.full + 1
        self.lanes = self.nb * tok_rows
        self.c = self.nyh * self.cap
        self.grp = self.nb * self.cap
        self.rows = self.nq * self.c
        self.msg = self.groups * self.grp
        self.pitch = pitch(self.msg)
        self.ntail = self.nyl // 2
        self.pairs = (self.cap + 1) // 2
        self.tail = -(-max(self.ntail * self.c, self.pairs * self.nz) // 8) * 8
        self.ret = self.full * self.grp + self.tail
        self.ret_pitch = pitch(self.ret)
        self.half_d = self.nyl * part_w
        self.pre = self.groups * tok_rows + 2 * picks
        self.fin = (self.full + 1) * tok_rows

    def device(self, x, yh, z, yl, core):
        return (((x * self.nyh + yh) * self.nz + z) * self.nyl + yl) * self.nc + core

    def column_groups(self):
        xs, yhs, zs, yls = map(range, (self.nx, self.nyh, self.nz, self.nyl))
        first = [[self.device(x, h, z, l, Y_CORE) for h in yhs for l in yls] for x in xs for z in zs]
        second = [
            [self.device(x, h, z, l, 1 - Y_CORE) for z in zs] for x in xs for h in yhs for l in yls
        ]
        return first + second

    def plane_groups(self):
        xs, yhs, zs, yls = map(range, (self.nx, self.nyh, self.nz, self.nyl))
        first = [[self.device(x, h, z, l, Y_CORE) for x in xs for z in zs] for h in yhs for l in yls]
        second = [[self.device(x, h, z, l, 1 - Y_CORE) for x in xs for h in yhs for l in yls] for z in zs]
        return first + second


def iota(shape, dim):
    return lax.broadcasted_iota(jnp.int32, shape, dim)


def call(kernel, outs, args, scratch=(), flops=0, spaces=None, limit=VMEM_LIMIT, out_spaces=None):
    vm = pl.BlockSpec(memory_space=pltpu.VMEM)
    spaces = spaces or {}
    size = sum(a.size * a.dtype.itemsize for a in args) + sum(
        jnp.dtype(o[1]).itemsize * functools.reduce(lambda a, b: a * b, o[0]) for o in outs
    )
    shapes = [jax.ShapeDtypeStruct(s, d) for s, d in outs]
    return pl.pallas_call(
        kernel,
        out_shape=shapes,
        in_specs=[spaces.get(k, vm) for k in range(len(args))],
        out_specs=[(out_spaces or {}).get(k, vm) for k in range(len(outs))],
        scratch_shapes=list(scratch),
        compiler_params=pltpu.CompilerParams(vmem_limit_bytes=limit),
        cost_estimate=pl.CostEstimate(flops=flops, bytes_accessed=size, transcendentals=0),
    )(*args)


def pack_kernel(p, *refs):
    out_ref, block_ref, sems = refs[4], refs[9], refs[10]
    x_ref, dy_ref, route_ref, gate_ref = refs[5:9]
    fetches = [
        pltpu.make_async_copy(refs[k], refs[5 + k], sems.at[k]) for k in range(4)
    ]
    for fetch in fetches:
        fetch.start()
    for fetch in fetches:
        fetch.wait()
    in_y = lax.axis_index("yh") * p.nyl + lax.axis_index("yl")
    block = jnp.where(lax.axis_index("core") == Y_CORE, in_y, lax.axis_index("z"))
    top = p.full * LANES
    low = (iota((HALF, LANES), 1) == iota((HALF, LANES), 0)).astype(BF)
    high = (iota((HALF, LANES), 1) == iota((HALF, LANES), 0) + HALF).astype(BF)
    mixed = jnp.dot(x_ref[:, top:], low, preferred_element_type=F32) + jnp.dot(
        dy_ref[:, top:], high, preferred_element_type=F32
    )
    lanes = (iota((p.tok, LANES), 1) == iota((p.tok, LANES), 0) + block * p.tok).astype(BF)
    meta = jnp.concatenate(
        [route_ref[...].astype(F32), gate_ref[...].astype(F32)], axis=0
    ).astype(BF)
    placed = jnp.dot(meta, lanes, preferred_element_type=F32).astype(BF)
    t = p.tok
    for j in range(p.full):
        block_ref[j * t : (j + 1) * t, :] = x_ref[:, j * LANES : (j + 1) * LANES]
        k = p.full + 1 + j
        block_ref[k * t : (k + 1) * t, :] = dy_ref[:, j * LANES : (j + 1) * LANES]
    block_ref[p.full * t : (p.full + 1) * t, :] = mixed.astype(BF)
    block_ref[p.groups * t :, :] = placed
    stores = [
        pltpu.make_async_copy(block_ref, out_ref.at[b], sems.at[4 + b]) for b in range(p.nb)
    ]
    for store in stores:
        store.start()
    for store in stores:
        store.wait()


def slot_target(p, first):
    r = iota((p.grp, p.lanes), 0)
    b = iota((p.grp, p.lanes), 1) // p.tok
    c = r % p.c
    in_y = jnp.where((r // p.c == b % p.nyl) & (c // p.cap == b // p.nyl), c % p.cap, -2)
    in_z = jnp.where(r % p.nz == b, r // p.nz, -2)
    return jnp.where(first, in_y, in_z).astype(F32)


def one_hot(p, ranks, target, weight=1.0):
    eq = ranks[:, None, :] == target[None, :, :]
    return jnp.where(eq, weight, 0.0).astype(F32).reshape(-1, p.lanes).astype(BF)


def dispatch_kernel(p, in_ref, out_ref, rank_ref, held, sems):
    first = lax.axis_index("core") == Y_CORE
    yh, z = lax.axis_index("yh"), lax.axis_index("z")
    t = p.tok
    meta = in_ref[0, p.groups * t :, :].astype(F32)
    for b in range(1, p.nb):
        meta = meta + in_ref[b, p.groups * t :, :].astype(F32)
    q = iota((p.nq, p.lanes), 0)
    in_y = ((q // p.nz) * p.nyh + yh) * p.nz + q % p.nz
    in_z = (q // p.nyl) * p.nz + z
    expert = jnp.where(first, in_y, in_z).astype(F32)
    hit = jnp.zeros((p.nq, p.lanes), F32)
    gate = jnp.zeros((p.nq, p.lanes), F32)
    for k in range(p.picks):
        same = meta[k : k + 1, : p.lanes] == expert
        hit = hit + jnp.where(same, 1.0, 0.0)
        gate = gate + jnp.where(same, meta[p.picks + k : p.picks + k + 1, : p.lanes], 0.0)
    a, b = iota((p.lanes, p.lanes), 0), iota((p.lanes, p.lanes), 1)
    before = jnp.where((a < b) & (a // t == b // t), 1.0, 0.0).astype(BF)
    rank = jnp.dot(hit.astype(BF), before, preferred_element_type=F32)
    ranks = jnp.where(hit > 0.5, rank, -1.0)
    rank_ref[...] = ranks
    target = slot_target(p, first)
    pick = one_hot(p, ranks, target)
    gate = jnp.broadcast_to(gate[:, None, :], (p.nq, p.grp, p.lanes))
    scaled = one_hot(p, ranks, target, gate)
    left = iota((p.nq * p.grp, LANES), 1) < HALF
    stores = []
    for g in range(p.groups):
        feats = in_ref[:, g * t : (g + 1) * t, :].reshape(p.lanes, LANES)
        rows = jnp.dot(pick if g <= p.full else scaled, feats, preferred_element_type=F32)
        if g == p.full:
            both = jnp.dot(scaled, feats, preferred_element_type=F32)
            rows = jnp.where(left, rows, both)
        at = slice(g * p.grp, (g + 1) * p.grp)
        held[:, at, :] = rows.astype(BF).reshape(p.nq, p.grp, LANES)
        store = pltpu.make_async_copy(held.at[:, at, :], out_ref.at[:, at, :], sems.at[g])
        store.start()
        stores.append(store)
    for store in stores:
        store.wait()


def project_kernel(p, in_ref, wgu_ref, wd_hbm, x_ref, pre_ref, send_ref, flat, dy, wd, sem):
    fetch = pltpu.make_async_copy(wd_hbm.at[: p.half_d], wd, sem)
    fetch.start()
    first = lax.axis_index("core") == Y_CORE

    def piece_in_y(group, yl):
        row = group * p.grp + yl * p.c
        return jnp.concatenate(
            [flat[pl.ds(row + c, p.nq, stride=p.pitch), :] for c in range(p.c)], axis=0
        )

    def blocks():
        for yh in range(p.nyh):
            for c in range(p.cap):
                for x in range(p.nx):
                    yield c, (x * p.nyh + yh) * p.nyl

    def piece_in_z(group, yl):
        rows = [(s + yl) * p.pitch + group * p.grp + c * p.nz for c, s in blocks()]
        return jnp.concatenate([flat[r : r + p.nz, :] for r in rows], axis=0)

    left = iota((p.rows, LANES), 1) < HALF

    def project(piece):
        for s in range(p.nq):
            flat[s * p.pitch : s * p.pitch + p.msg, :] = in_ref[s].astype(F32)
        for j in range(p.full):
            for yl in range(p.nyl):
                at = (j * p.nyl + yl) * LANES
                x_ref[:, at : at + LANES] = piece(j, yl).astype(BF)
                dy[:, at : at + LANES] = piece(p.full + 1 + j, yl).astype(BF)
        for u in range(p.ntail):
            at = (p.full * p.nyl + u) * LANES
            a = piece(p.full, 2 * u)
            b = piece(p.full, 2 * u + 1)
            x_ref[:, at : at + LANES] = jnp.where(left, a, pltpu.roll(b, HALF, 1)).astype(BF)
            dy[:, at : at + LANES] = jnp.where(left, pltpu.roll(a, HALF, 1), b).astype(BF)
        pre = jnp.dot(x_ref[...], wgu_ref[...], preferred_element_type=F32)
        fetch.wait()
        back = jnp.dot(dy[...], wd[...], preferred_element_type=F32)
        two, three = 2 * LANES, 3 * LANES
        pre_ref[:, :two] = pre[:, :two]
        pre_ref[:, two:three] = back[:, :LANES]
        pre_ref[:, three : three + two] = pre[:, two:]
        pre_ref[:, three + two :] = back[:, LANES:]
        send_ref[...] = pre_ref[...].astype(BF)

    @pl.when(first)
    def _():
        project(piece_in_y)

    @pl.when(jnp.logical_not(first))
    def _():
        project(piece_in_z)


def stash_kernel(in_ref, out_ref, sem):
    copy = pltpu.make_async_copy(in_ref, out_ref.at[: in_ref.shape[0]], sem)
    copy.start()
    copy.wait()


def back_kernel(p, pre_ref, got_ref, wgu_ref, out_ref, d_ref, flat, held, sems):
    two, three = 2 * LANES, 3 * LANES
    nt = (((1,), (1,)), ((), ()))
    tail = p.full * p.grp
    chunks = p.full * p.nyl
    left = iota((p.nz, LANES), 1) < HALF
    for k in range(2):
        mine, theirs = k * three, (1 - k) * three

        def whole(at):
            own = pre_ref[:, mine + at : mine + at + LANES]
            return own + got_ref[:, theirs + at : theirs + at + LANES].astype(F32)

        pre_gate, pre_up, scaled = whole(0), whole(LANES), whole(two)
        sig = 1.0 / (1.0 + jnp.exp(-pre_gate))
        d_gate = scaled * pre_up * sig * (1.0 + pre_gate * (1.0 - sig))
        d_ref[:, k * two : k * two + LANES] = d_gate.astype(BF)
        d_ref[:, k * two + LANES : (k + 1) * two] = (scaled * pre_gate * sig).astype(BF)

    def part(k):
        at = k * LANES
        return lax.dot_general(
            d_ref[...], wgu_ref[at : at + LANES, :], nt, preferred_element_type=F32
        )

    def put_in_y(k, value):
        base = k * p.c if k < chunks else tail + (k - chunks) * p.c
        for c in range(p.c):
            flat[pl.ds(base + c, p.nq, stride=p.ret_pitch), :] = value[c * p.nq : (c + 1) * p.nq, :]

    def put_in_z(k, value):
        def block(yh, c, x):
            at = ((yh * p.cap + c) * p.nx + x) * p.nz
            return value[at : at + p.nz, :]

        for yh in range(p.nyh):
            for x in range(p.nx):
                s = (x * p.nyh + yh) * p.nyl
                if k < chunks:
                    for c in range(p.cap):
                        row = (s + k % p.nyl) * p.ret_pitch + k // p.nyl * p.grp + c * p.nz
                        flat[row : row + p.nz, :] = block(yh, c, x)
                    continue
                for c in range(0, p.cap, 2):
                    one = block(yh, c, x)
                    two = block(yh, c + 1, x) if c + 1 < p.cap else one
                    ends = (
                        jnp.where(left, one, pltpu.roll(two, HALF, 1)),
                        jnp.where(left, pltpu.roll(one, HALF, 1), two),
                    )
                    for h in range(2):
                        row = (s + 2 * (k - chunks) + h) * p.ret_pitch + tail + c // 2 * p.nz
                        flat[row : row + p.nz, :] = ends[h]

    def rows_of(g):
        return slice(g * p.grp, (g + 1) * p.grp if g < p.full else p.ret)

    def store(g):
        at = rows_of(g)
        for s in range(p.nq):
            base = s * p.ret_pitch
            held[s, at, :] = flat[base + at.start : base + at.stop, :].astype(BF)
        copy = pltpu.make_async_copy(held.at[:, at, :], out_ref.at[:, at, :], sems.at[g])
        copy.start()
        return copy

    def run(put):
        copies = []
        for g in range(p.full):
            for yl in range(p.nyl):
                put(g * p.nyl + yl, part(g * p.nyl + yl))
            copies.append(store(g))
        for u in range(p.ntail):
            put(chunks + u, part(chunks + u))
        copies.append(store(p.full))
        for copy in copies:
            copy.wait()

    first = lax.axis_index("core") == Y_CORE

    @pl.when(first)
    def _():
        for r in range(tail + p.ntail * p.c, tail + p.tail):
            flat[pl.ds(r, p.nq, stride=p.ret_pitch), :] = jnp.zeros((p.nq, LANES), F32)
        run(put_in_y)

    @pl.when(jnp.logical_not(first))
    def _():
        run(put_in_z)


def combine_kernel(p, in_ref, pick_ref, ends_ref, out_ref):
    t = p.tok
    first = lax.axis_index("core") == Y_CORE
    for g in range(p.full):
        rows = in_ref[:, g * p.grp : (g + 1) * p.grp, :].reshape(p.nq * p.grp, LANES)
        total = jnp.dot(pick_ref[...], rows, preferred_element_type=F32)
        out_ref[:, g * t : (g + 1) * t, :] = total.astype(BF).reshape(p.nb, t, LANES)
    tail = p.full * p.grp

    def tail_total(lanes, start, rows):
        rows = in_ref[:, tail + start : tail + start + rows, :].reshape(-1, LANES)
        return jnp.dot(ends_ref[:, lanes], rows, preferred_element_type=F32)

    @pl.when(first)
    def _():
        last = tail_total(slice(0, p.nq * p.tail), 0, p.tail)
        for b in range(p.nb):
            src = (b // p.nyl) * p.nyl + (b % p.nyl) // 2
            out_ref[b, p.full * t :, :] = last[src * t : (src + 1) * t, :].astype(BF)

    @pl.when(jnp.logical_not(first))
    def _():
        sides = [None, None]
        n = p.nq * p.nz
        for c in range(p.cap):
            part = tail_total(slice(c * n, (c + 1) * n), c // 2 * p.nz, p.nz)
            sides[c % 2] = part if sides[c % 2] is None else sides[c % 2] + part
        last = sides[0] + pltpu.roll(sides[1], HALF, 1)
        out_ref[:, p.full * t :, :] = last.astype(BF).reshape(p.nb, t, LANES)


def finish_kernel(p, in_ref, out_ref):
    odd = jnp.where(lax.axis_index("core") == Y_CORE, lax.axis_index("yl") % 2, 0)
    total = in_ref[0].astype(F32)
    for b in range(1, p.nb):
        total = total + in_ref[b].astype(F32)
    t = p.tok
    for j in range(p.full):
        out_ref[:, j * LANES : (j + 1) * LANES] = total[j * t : (j + 1) * t, :].astype(BF)
    tail = total[p.full * t :, :]
    tail = jnp.where(odd == 1, pltpu.roll(tail, HALF, 1), tail)
    out_ref[:, p.full * LANES :] = tail[:, :HALF].astype(BF)


def grads_kernel(p, x_ref, d_ref, rank_ref, mine_ref, other_ref, pick_ref, ends_ref):
    first = lax.axis_index("core") == Y_CORE
    eq = rank_ref[...][:, None, :] == slot_target(p, first)[None, :, :]
    pick = jnp.where(eq, 1.0, 0.0).astype(F32)

    def turned(rows):
        return rows.reshape(-1, p.lanes).T.astype(BF)

    pick_ref[...] = turned(pick)

    @pl.when(first)
    def _():
        ends_ref[:, : p.nq * p.tail] = turned(pick[:, : p.tail, :])

    @pl.when(jnp.logical_not(first))
    def _():
        n = p.nq * p.nz
        for c in range(p.cap):
            ends_ref[:, c * n : (c + 1) * n] = turned(pick[:, c * p.nz : (c + 1) * p.nz, :])

    tn = (((0,), (0,)), ((), ()))

    def put(yl, at, size, src, got, k):
        mine_ref[k, yl, at : at + size, :] = got[src : src + size, k * LANES : (k + 1) * LANES]

    def put_other(yl, at, size, src, got):
        other_ref[yl, at : at + size, :] = got[src : src + size, :]

    for k in range(p.full * p.nyl + p.ntail):
        x = x_ref[:, k * LANES : (k + 1) * LANES]
        both = lax.dot_general(x, d_ref[...], tn, preferred_element_type=F32).astype(BF)
        mine, other = both[:, : 2 * LANES], both[:, 2 * LANES :]
        if k < p.full * p.nyl:
            spots = [(k % p.nyl, (k // p.nyl) * LANES, LANES, 0)]
        else:
            u = k - p.full * p.nyl
            spots = [(2 * u + h, p.full * LANES, HALF, h * HALF) for h in range(2)]
        for spot in spots:
            put(*spot, mine, 0)
            put(*spot, mine, 1)
            put_other(*spot, other)


def assemble_kernel(p, mine_ref, got_ref, gate_ref, up_ref):
    core = lax.axis_index("core")
    for yl in range(p.nyl):
        gate_ref[yl, core] = mine_ref[0, yl]
        up_ref[yl, core] = mine_ref[1, yl]
        gate_ref[yl, 1 - core] = got_ref[yl, :, :LANES]
        up_ref[yl, 1 - core] = got_ref[yl, :, LANES:]


def lane_tiles(p, w):
    top = p.full * LANES
    n = w.shape[-1]
    tiles = w[:, :top].reshape(p.nyl, p.full, LANES, n).transpose(1, 0, 2, 3).reshape(-1, n)
    return jnp.concatenate([tiles, w[:, top:].reshape(-1, n)], axis=0)


def body(sizes, *args):
    return program(sizes, *args)


def program(sizes, tokens, grad_out, gate_weights, routing, w_gate, w_up, w_down):
    p = Plan(sizes, *routing.shape, tokens.shape[1])
    swap = [(0, 1), (1, 0)]
    core = lax.axis_index("core")
    bind = functools.partial

    def exchange(v):
        return lax.ppermute(v, "core", swap)

    def all_to_all(v, groups):
        return lax.all_to_all(
            v, AXES, split_axis=0, concat_axis=0, axis_index_groups=groups, tiled=True
        )

    column_groups, plane_groups = p.column_groups(), p.plane_groups()

    (pre,) = call(
        bind(pack_kernel, p),
        [((p.nb, p.pre, LANES), BF)],
        (tokens, grad_out, routing.T, gate_weights.T),
        scratch=[
            pltpu.VMEM(tokens.shape, BF),
            pltpu.VMEM(grad_out.shape, BF),
            pltpu.VMEM(routing.shape[::-1], routing.dtype),
            pltpu.VMEM(gate_weights.shape[::-1], BF),
            pltpu.VMEM((p.pre, LANES), BF),
            pltpu.SemaphoreType.DMA((4 + p.nb,)),
        ],
        out_spaces={0: HBM},
        spaces={k: HBM for k in range(4)},
        limit=VMEM_ALL,
    )
    column = all_to_all(pre, column_groups)

    w_gate, w_up, w_down = lax.optimization_barrier((w_gate, w_up, w_down, pre))[:3]
    shape = (p.nyl, p.nc, p.part_w, LANES)
    weights = jnp.stack(
        [w_gate[0].reshape(shape), w_up[0].reshape(shape), w_down[0].T.reshape(shape)]
    )
    mine = lax.dynamic_index_in_dim(weights, core, axis=2, keepdims=False)
    other = lax.dynamic_index_in_dim(weights, 1 - core, axis=2, keepdims=False)
    theirs = exchange(other)
    wgu = lane_tiles(p, jnp.concatenate([mine[0], mine[1], theirs[0], theirs[1]], axis=-1))
    wd = lane_tiles(p, jnp.concatenate([mine[2], theirs[2]], axis=-1))
    (wd,) = call(
        stash_kernel,
        [((STASH_ROWS, 2 * LANES), BF)],
        (wd,),
        scratch=[pltpu.SemaphoreType.DMA],
        out_spaces={0: HBM},
        limit=3 * VMEM_LIMIT,
    )

    sent, ranks = call(
        bind(dispatch_kernel, p),
        [((p.nq, p.msg, LANES), BF), ((p.nq, p.lanes), F32)],
        (column,),
        scratch=[
            pltpu.VMEM((p.nq, p.msg, LANES), BF),
            pltpu.SemaphoreType.DMA((p.groups,)),
        ],
        out_spaces={0: HBM},
    )
    received = all_to_all(sent, plane_groups)
    rows_x, partial, crossing = call(
        bind(project_kernel, p),
        [
            ((p.rows, p.half_d), BF),
            ((p.rows, 6 * LANES), F32),
            ((p.rows, 6 * LANES), BF),
        ],
        (received, wgu, wd),
        scratch=[
            pltpu.VMEM(((p.nq + 1) * p.pitch, LANES), F32),
            pltpu.VMEM((p.rows, p.half_d), BF),
            pltpu.VMEM((p.half_d, 2 * LANES), BF),
            pltpu.SemaphoreType.DMA,
        ],
        spaces={2: HBM},
        limit=3 * VMEM_LIMIT,
    )
    back, d_all = call(
        bind(back_kernel, p),
        [((p.nq, p.ret, LANES), BF), ((p.rows, 4 * LANES), BF)],
        (partial, exchange(crossing), wgu),
        scratch=[
            pltpu.VMEM(((p.nq + 1) * p.ret_pitch, LANES), F32),
            pltpu.VMEM((p.nq, p.ret, LANES), BF),
            pltpu.SemaphoreType.DMA((p.full + 1,)),
        ],
        out_spaces={0: HBM},
    )
    returned = all_to_all(back, plane_groups)
    rows_x, d_all = lax.optimization_barrier((rows_x, d_all, back))[:2]
    chosen = ((p.lanes, p.nq * p.grp), BF)
    grad_mine, grad_other, pick, ends = call(
        bind(grads_kernel, p),
        [((2, p.nyl, p.part_w, LANES), BF), ((p.nyl, p.part_w, 2 * LANES), BF), chosen, chosen],
        (rows_x, d_all, ranks),
    )
    grad_got = exchange(grad_other)
    (share,) = call(bind(combine_kernel, p), [((p.nb, p.fin, LANES), BF)], (returned, pick, ends))
    last = all_to_all(share, column_groups)
    grad_mine, grad_got = lax.optimization_barrier((grad_mine, grad_got, share))[:2]
    grad_g, grad_u = call(
        bind(assemble_kernel, p), [(shape, BF), (shape, BF)], (grad_mine, grad_got)
    )
    (grad_tokens,) = call(bind(finish_kernel, p), [((p.tok, p.part_w), BF)], (last,))
    out = (1, p.nyl * p.nc * p.part_w, LANES)
    return grad_tokens, grad_g.reshape(out), grad_u.reshape(out)


def solution(mesh):
    sizes = axis_sizes(mesh.shape["expert"], mesh.shape["tensor"])
    inner = Mesh(mesh.devices.reshape(sizes), AXES)
    ex, te = AXES[:3], AXES[3:]
    placed = (
        P(ex, te),
        P(ex, te),
        P(ex, None),
        P(ex, None),
        P(ex, None, te),
        P(ex, None, te),
        P(ex, te, None),
    )
    return jax.shard_map(
        functools.partial(body, sizes),
        mesh=inner,
        in_specs=placed,
        out_specs=(P(ex, te), P(ex, None, te), P(ex, None, te)),
        check_vma=False,
    )
```
